256 devices in a mesh: az: 16 (over z, x_hi), rad: 16 (over y, x_lo, core).
Axes of the slice: x: 4 (x_hi: 2, x_lo: 2; x = x_hi * 2 + x_lo), y: 4, z: 8, core: 2. Of those that a mesh axis runs over, the one named last changes fastest.
Arguments:
- fields: float32 [8, 256, 512, 128], P(None, 'rad', 'az'), as said below
- offsets: int32 [256], replicated, may hold values from 0 to 511
- boundary_shift: int32 [1], replicated, may hold values from 0 to 511
Outputs:
- advanced: float32 [8, 256, 512, 128], P(None, 'rad', 'az')
The draws below stay inside these ranges and needn't reach their ends.
Inputs may be any that keep to these rules, and one draw needn't show every extreme that they name: Each cell of fields is a conserved state whose density and implied pressure lie between 0.5 and 2; velocities stay under 1.8 and field components under 0.9 in magnitude.
All inputs are finite; a program needn't handle non-finite values.
Results may differ from the reference program's by a relative error of at most 0.0003.
Values sent between devices are 32-bit elements; how exact they have to be, the bound alone decides.
No kernel may reach another device: no remote copies, remote signals or barrier semaphores. Data moves between devices by JAX's collectives and lax.ppermute only.
A program may use at most 192 MiB of HBM per device.

```python
import jax
import jax.numpy as jnp
from jax import lax

CX = 16
NX = 256
NY = 512
NZ = 128
N_RAD = 16


GAMMA_RATIO = 5.0 / 3.0


def draw_fields(key, part):
    subkeys = jax.random.split(key, 4)
    grid_shape = (NX, NY, NZ)
    radial_ramp = 1.0 + 2.0 * jnp.arange(NX, dtype=jnp.float32)[:, None, None] / max(NX - 1, 1)
    density = jnp.exp(jax.random.uniform(subkeys[0], grid_shape, jnp.float32, -0.69, 0.69))
    pressure = jnp.exp(jax.random.uniform(subkeys[1], grid_shape, jnp.float32, -0.69, 0.69))
    velocity = jnp.clip(0.2 * jax.random.normal(subkeys[2], (3,) + grid_shape, jnp.float32), -0.6, 0.6) * radial_ramp
    magnetic = jnp.clip(0.3 * jax.random.normal(subkeys[3], (3,) + grid_shape, jnp.float32), -0.9, 0.9)
    momentum = density * velocity
    energy = pressure / (GAMMA_RATIO - 1.0) + 0.5 * density * jnp.sum(velocity * velocity, axis=0) + 0.5 * jnp.sum(magnetic * magnetic, axis=0)
    return jnp.concatenate([density[None], momentum, energy[None], magnetic], axis=0).astype(jnp.float32)


def with_ends(array, key, smallest, high):
    longest = array.shape.index(max(array.shape))
    spots = []
    for shift in (0, 1):
        where = [jax.random.randint(jax.random.fold_in(key, axis), (), 0, length) for axis, length in enumerate(array.shape)]
        where[longest] = (where[longest] + shift) % array.shape[longest]
        spots.append(tuple(where))
    return array.at[spots[0]].set(smallest).at[spots[1]].set(high)


def setup_inputs(seed: int = 0) -> dict:
    key_of = jax.random.split(jax.random.key(seed), 4)
    return {
        "fields": draw_fields(jax.random.fold_in(key_of[3], 71), 0),
        "offsets": with_ends(jax.random.randint(key_of[1], (NX,), 0, NY), jax.random.fold_in(key_of[1], 1), 0, NY - 1).astype(jnp.int32),
        "boundary_shift": jax.random.randint(key_of[2], (1,), 0, NY).astype(jnp.int32),
    }


GAMMA_RATIO = 5.0 / 3.0
CFL_NUMBER = 0.4
OMEGA_RATE = 1.0
SHEAR_RATE = 1.5

def primitive(state):
    density = state[0]
    inverse = 1.0 / density
    speed_x = state[1] * inverse
    speed_y = state[2] * inverse
    speed_z = state[3] * inverse
    kinetic = 0.5 * density * (speed_x * speed_x + speed_y * speed_y + speed_z * speed_z)
    magnetic = 0.5 * (state[5] * state[5] + state[6] * state[6] + state[7] * state[7])
    pressure = (GAMMA_RATIO - 1.0) * (state[4] - kinetic - magnetic)
    return (density, speed_x, speed_y, speed_z, pressure, state[5], state[6], state[7])

def fast_speed(density, pressure, normal_field, field_sq):
    sound = (GAMMA_RATIO * pressure + field_sq) / density
    spread = jnp.maximum(sound * sound - 4.0 * GAMMA_RATIO * pressure * normal_field * normal_field / (density * density), 0.0)
    return jnp.sqrt(0.5 * (sound + jnp.sqrt(spread)))

def cell_speed(primitives):
    field_sq = primitives[5] * primitives[5] + primitives[6] * primitives[6] + primitives[7] * primitives[7]
    total = jnp.abs(primitives[1]) + fast_speed(primitives[0], primitives[4], primitives[5], field_sq)
    total = total + jnp.abs(primitives[2]) + fast_speed(primitives[0], primitives[4], primitives[6], field_sq)
    total = total + jnp.abs(primitives[3]) + fast_speed(primitives[0], primitives[4], primitives[7], field_sq)
    return total

def minmod(first_diff, second_diff):
    return 0.5 * (jnp.sign(first_diff) + jnp.sign(second_diff)) * jnp.minimum(jnp.abs(first_diff), jnp.abs(second_diff))

def take_range(values, start_at, stop_at, along):
    return lax.slice_in_dim(values, start_at, stop_at, axis=along)

def side_terms(values, normal_field):
    density, normal_speed, trans_speed, other_speed, pressure = (values[0], values[1], values[2], values[3], values[4])
    trans_field, other_field = (values[6], values[7])
    field_sq = normal_field * normal_field + trans_field * trans_field + other_field * other_field
    total_press = pressure + 0.5 * field_sq
    energy = pressure / (GAMMA_RATIO - 1.0) + 0.5 * density * (normal_speed * normal_speed + trans_speed * trans_speed + other_speed * other_speed) + 0.5 * field_sq
    field_work = normal_speed * normal_field + trans_speed * trans_field + other_speed * other_field
    conserved = (density, density * normal_speed, density * trans_speed, density * other_speed, energy, normal_field, trans_field, other_field)
    fluxes = (density * normal_speed, density * normal_speed * normal_speed + total_press - normal_field * normal_field, density * normal_speed * trans_speed - normal_field * trans_field, density * normal_speed * other_speed - normal_field * other_field, (energy + total_press) * normal_speed - normal_field * field_work, jnp.zeros_like(density), trans_field * normal_speed - normal_field * trans_speed, other_field * normal_speed - normal_field * other_speed)
    signal = fast_speed(density, pressure, normal_field, field_sq)
    return (conserved, fluxes, total_press, energy, field_work, signal)

def star_state(values, energy, total_press, field_work, normal_field, outer, middle, star_press):
    density, normal_speed, trans_speed, other_speed = (values[0], values[1], values[2], values[3])
    trans_field, other_field = (values[6], values[7])
    relative = outer - normal_speed
    distance = outer - middle
    star_density = density * relative / distance
    product = density * relative * distance
    divisor = jnp.maximum(product - normal_field * normal_field, 0.5 * product)
    trans_star = trans_speed - normal_field * trans_field * (middle - normal_speed) / divisor
    other_star = other_speed - normal_field * other_field * (middle - normal_speed) / divisor
    factor = (density * relative * relative - normal_field * normal_field) / divisor
    trans_bstar = trans_field * factor
    other_bstar = other_field * factor
    star_work = middle * normal_field + trans_star * trans_bstar + other_star * other_bstar
    star_energy = (relative * energy - total_press * normal_speed + star_press * middle + normal_field * (field_work - star_work)) / distance
    return (star_density, trans_star, other_star, trans_bstar, other_bstar, star_work, star_energy)

def hlld_flux(left_values, right_values):
    normal_field = 0.5 * (left_values[5] + right_values[5])
    cons_left, flux_left, press_left, energy_left, work_left, signal_left = side_terms(left_values, normal_field)
    cons_right, flux_right, press_right, energy_right, work_right, signal_right = side_terms(right_values, normal_field)
    fastest = jnp.maximum(signal_left, signal_right)
    lower = jnp.minimum(left_values[1], right_values[1]) - fastest
    upper = jnp.maximum(left_values[1], right_values[1]) + fastest
    mass_left = left_values[0] * (lower - left_values[1])
    mass_right = right_values[0] * (upper - right_values[1])
    guess = (mass_right * right_values[1] - mass_left * left_values[1] - press_right + press_left) / (mass_right - mass_left)
    margin = 0.1 * (upper - lower)
    middle = jnp.clip(guess, lower + margin, upper - margin)
    star_press = press_left + mass_left * (middle - left_values[1])
    dens_left, trans_left, other_left, tfield_left, ofield_left, swork_left, senergy_left = star_state(left_values, energy_left, press_left, work_left, normal_field, lower, middle, star_press)
    dens_right, trans_right, other_right, tfield_right, ofield_right, swork_right, senergy_right = star_state(right_values, energy_right, press_right, work_right, normal_field, upper, middle, star_press)
    root_left = jnp.sqrt(dens_left)
    root_right = jnp.sqrt(dens_right)
    sign_field = jnp.sign(normal_field)
    root_sum = root_left + root_right
    trans_double = (root_left * trans_left + root_right * trans_right + (tfield_right - tfield_left) * sign_field) / root_sum
    other_double = (root_left * other_left + root_right * other_right + (ofield_right - ofield_left) * sign_field) / root_sum
    tfield_double = (root_left * tfield_right + root_right * tfield_left + root_left * root_right * (trans_right - trans_left) * sign_field) / root_sum
    ofield_double = (root_left * ofield_right + root_right * ofield_left + root_left * root_right * (other_right - other_left) * sign_field) / root_sum
    double_work = middle * normal_field + trans_double * tfield_double + other_double * ofield_double
    denergy_left = senergy_left - root_left * (swork_left - double_work) * sign_field
    denergy_right = senergy_right + root_right * (swork_right - double_work) * sign_field
    inner_left = middle - jnp.abs(normal_field) / root_left
    inner_right = middle + jnp.abs(normal_field) / root_right
    star_cons_left = (dens_left, dens_left * middle, dens_left * trans_left, dens_left * other_left, senergy_left, normal_field, tfield_left, ofield_left)
    star_cons_right = (dens_right, dens_right * middle, dens_right * trans_right, dens_right * other_right, senergy_right, normal_field, tfield_right, ofield_right)
    double_cons_left = (dens_left, dens_left * middle, dens_left * trans_double, dens_left * other_double, denergy_left, normal_field, tfield_double, ofield_double)
    double_cons_right = (dens_right, dens_right * middle, dens_right * trans_double, dens_right * other_double, denergy_right, normal_field, tfield_double, ofield_double)
    outcome = []
    for component in range(8):
        star_left = flux_left[component] + lower * (star_cons_left[component] - cons_left[component])
        double_left = star_left + inner_left * (double_cons_left[component] - star_cons_left[component])
        star_right = flux_right[component] + upper * (star_cons_right[component] - cons_right[component])
        double_right = star_right + inner_right * (double_cons_right[component] - star_cons_right[component])
        chosen = jnp.where(lower > 0, flux_left[component], jnp.where(inner_left > 0, star_left, jnp.where(middle > 0, double_left, jnp.where(inner_right > 0, double_right, jnp.where(upper > 0, star_right, flux_right[component])))))
        outcome.append(chosen)
    outcome[5] = jnp.zeros_like(outcome[0])
    return outcome

def direction_divergence(primitives, along, normal_order):
    mapping = (0, normal_order[0], normal_order[1], normal_order[2], 4, normal_order[0] + 4, normal_order[1] + 4, normal_order[2] + 4)
    left_faces = []
    right_faces = []
    for component in range(8):
        values = primitives[mapping[component]]
        length = values.shape[along]
        cell_count = length - 4
        differences = take_range(values, 1, length, along) - take_range(values, 0, length - 1, along)
        slopes = minmod(take_range(differences, 0, length - 2, along), take_range(differences, 1, length - 1, along))
        centres = take_range(values, 1, length - 1, along)
        left_faces.append(take_range(centres, 0, cell_count + 1, along) + 0.5 * take_range(slopes, 0, cell_count + 1, along))
        right_faces.append(take_range(centres, 1, cell_count + 2, along) - 0.5 * take_range(slopes, 1, cell_count + 2, along))
    face_fluxes = hlld_flux(left_faces, right_faces)
    result = [None] * 8
    for component in range(8):
        face_values = face_fluxes[component]
        length = face_values.shape[along]
        result[mapping[component]] = take_range(face_values, 1, length, along) - take_range(face_values, 0, length - 1, along)
    return result

def advance(radial_padded, azimuthal_padded, remapped, time_step):
    radial_div = direction_divergence(primitive(radial_padded), 0, (1, 2, 3))
    azimuthal_div = direction_divergence(primitive(azimuthal_padded), 1, (2, 3, 1))
    vertical_padded = jnp.concatenate([remapped[..., -2:], remapped, remapped[..., :2]], axis=3)
    vertical_div = direction_divergence(primitive(vertical_padded), 2, (3, 1, 2))
    gains = [0.0, 2.0 * OMEGA_RATE * remapped[2], -(2.0 - SHEAR_RATE) * OMEGA_RATE * remapped[1], 0.0, SHEAR_RATE * OMEGA_RATE * (remapped[1] * remapped[2] / remapped[0] - remapped[5] * remapped[6]), 0.0, -SHEAR_RATE * OMEGA_RATE * remapped[5], 0.0]
    outcome = []
    for component in range(8):
        change = radial_div[component] + azimuthal_div[component] + vertical_div[component]
        outcome.append(remapped[component] - time_step * change + time_step * gains[component])
    return jnp.stack(outcome)

def reference(fields, offsets, boundary_shift):
    radial_cells = fields.shape[1]
    loop_cells = fields.shape[2]
    depth_cells = fields.shape[3]
    amount = jnp.mod(offsets, loop_cells).astype(jnp.int32)
    positions = jnp.mod(jnp.arange(loop_cells, dtype=jnp.int32)[None, :] - amount[:, None], loop_cells).astype(jnp.int32)
    remapped_all = jnp.take_along_axis(fields, positions[None, :, :, None], axis=2)
    shear_cells = boundary_shift[0]
    lower_ghost = jnp.roll(remapped_all[:, radial_cells - 2:], shear_cells, axis=2)
    upper_ghost = jnp.roll(remapped_all[:, :2], -shear_cells, axis=2)
    radial_all = jnp.concatenate([lower_ghost, remapped_all, upper_ghost], axis=1)

    def block_peak(block_index):
        piece = lax.dynamic_slice_in_dim(fields, block_index * CX, CX, axis=1)
        return jnp.max(cell_speed(primitive(piece)))
    block_indices = jnp.arange(N_RAD, dtype=jnp.int32)
    global_peak = jnp.max(lax.map(block_peak, block_indices))
    time_step = CFL_NUMBER / global_peak

    def block_update(block_index):
        window = lax.dynamic_slice_in_dim(radial_all, block_index * CX, CX + 4, axis=1)
        remapped = window[:, 2:CX + 2]
        azimuthal_padded = jnp.concatenate([remapped[:, :, -2:], remapped, remapped[:, :, :2]], axis=2)
        return advance(window, azimuthal_padded, remapped, time_step)
    blocks = lax.map(block_update, block_indices)
    return jnp.moveaxis(blocks, 1, 0).reshape(8, radial_cells, loop_cells, depth_cells)
```

```python
import functools

import jax
import jax.numpy as jnp
from jax import lax
from jax.experimental import pallas as pl
from jax.experimental.pallas import tpu as pltpu
from jax.sharding import Mesh
from jax.sharding import PartitionSpec as P

AZ = ("az_0", "az_1")
RAD = ("rad_0", "rad_1", "rad_2")

GAMMA = 5.0 / 3.0
CFL_NUMBER = 0.4
OMEGA = 1.0
SHEAR = 1.5

FIELDS = 8
ROWS = 16
CELLS = 32
RING = 512
DEPTH = 128
GROUPS = 16
HOLDERS = 16
UNITS = 8
PAIRS = (0, 7, 1, 6, 2, 5, 3, 4)
EXTRA = UNITS * CELLS
PEAK = EXTRA + CELLS
LINES = PEAK + 8
TINY = 1e-30
VMEM = pl.BlockSpec(memory_space=pltpu.VMEM)
SMEM = pl.BlockSpec(memory_space=pltpu.SMEM)
HBM = pl.BlockSpec(memory_space=pl.ANY)
MIB = 1024 * 1024


def passed_along(array, axis, by):
    devices = lax.axis_size(axis)
    return lax.ppermute(array, axis, [(i, (i + by) % devices) for i in range(devices)])


def to_primitive(state):
    density = state[0]
    inverse = 1.0 / density
    vx = state[1] * inverse
    vy = state[2] * inverse
    vz = state[3] * inverse
    kinetic = 0.5 * (state[1] * vx + state[2] * vy + state[3] * vz)
    magnetic = 0.5 * (state[5] * state[5] + state[6] * state[6] + state[7] * state[7])
    pressure = (GAMMA - 1.0) * (state[4] - kinetic - magnetic)
    return (density, vx, vy, vz, pressure, state[5], state[6], state[7])


def fast_speed(density, pressure, normal_field, field_sq):
    sound = (GAMMA * pressure + field_sq) / density
    spread = jnp.maximum(
        sound * sound
        - 4.0 * GAMMA * pressure * normal_field * normal_field / (density * density),
        0.0,
    )
    return jnp.sqrt(0.5 * (sound + jnp.sqrt(spread)))


def cell_speed(prim):
    field_sq = prim[5] * prim[5] + prim[6] * prim[6] + prim[7] * prim[7]
    total = jnp.abs(prim[1]) + fast_speed(prim[0], prim[4], prim[5], field_sq)
    total = total + jnp.abs(prim[2]) + fast_speed(prim[0], prim[4], prim[6], field_sq)
    return total + jnp.abs(prim[3]) + fast_speed(prim[0], prim[4], prim[7], field_sq)


def half_slope(before, after):
    return 0.5 * jnp.minimum(
        jnp.maximum(after, jnp.minimum(before, 0.0)), jnp.maximum(before, 0.0)
    )


def hlld(left, right):
    rl, ul, tl, wl, pl_, nl, btl, bwl = left
    rr, ur, tr, wr, pr_, nr, btr, bwr = right
    bn = 0.5 * (nl + nr)
    bn2 = bn * bn

    def signal(p, bt, bw):
        b2 = bn2 + bt * bt + bw * bw
        gp = GAMMA * p
        h = gp + b2
        square = jnp.maximum(h * h - 4.0 * (gp * bn2), TINY)
        return h + square * lax.rsqrt(square), p + 0.5 * b2

    sig_l, ptl = signal(pl_, btl, bwl)
    sig_r, ptr = signal(pr_, btr, bwr)
    inv_rr = 1.0 / (rl * rr)
    square = (0.5 * inv_rr) * jnp.maximum(sig_l * rr, sig_r * rl)
    fastest = square * lax.rsqrt(square)
    lower = jnp.minimum(ul, ur) - fastest
    upper = jnp.maximum(ul, ur) + fastest
    rel_l = lower - ul
    rel_r = upper - ur
    ml = rl * rel_l
    mr = rr * rel_r
    guess = (mr * ur - ml * ul - ptr + ptl) / (mr - ml)
    margin = 0.1 * (upper - lower)
    sm = jnp.minimum(jnp.maximum(guess, lower + margin), upper - margin)
    press_star = ptl + ml * (sm - ul)

    def star(m, rel, outer, u, t, w, bt, bw):
        dist = outer - sm
        inv_dist = 1.0 / dist
        product = m * dist
        inv_div = 1.0 / jnp.maximum(product - bn2, 0.5 * product)
        k = bn * (sm - u) * inv_div
        factor = (m * rel - bn2) * inv_div
        dens = m * inv_dist
        inv_root = lax.rsqrt(dens)
        return (inv_dist, dens, dens * inv_root, inv_root,
                t - bt * k, w - bw * k, bt * factor, bw * factor)

    idl, dl, ql, iql, tsl, wsl, btsl, bwsl = star(ml, rel_l, lower, ul, tl, wl, btl, bwl)
    idr, dr, qr, iqr, tsr, wsr, btsr, bwsr = star(mr, rel_r, upper, ur, tr, wr, btr, bwr)
    sg = jnp.where(bn < 0.0, -1.0, 1.0)
    inv_sum = 1.0 / (ql + qr)
    al = ql * inv_sum
    ar = qr * inv_sum
    sgs = sg * inv_sum
    qqs = ql * ar * sg
    t2 = al * tsl + ar * tsr + (btsr - btsl) * sgs
    w2 = al * wsl + ar * wsr + (bwsr - bwsl) * sgs
    bt2 = al * btsr + ar * btsl + qqs * (tsr - tsl)
    bw2 = al * bwsr + ar * bwsl + qqs * (wsr - wsl)

    pos = sm > 0.0

    def pick(a, b):
        return jnp.where(pos, a, b)

    r, u, t, w, p = pick(rl, rr), pick(ul, ur), pick(tl, tr), pick(wl, wr), pick(pl_, pr_)
    bt, bw, pt, outer = pick(btl, btr), pick(bwl, bwr), pick(ptl, ptr), pick(lower, upper)
    rel, inv_dist, dens = pick(rel_l, rel_r), pick(idl, idr), pick(dl, dr)
    ts, ws, bts, bws = pick(tsl, tsr), pick(wsl, wsr), pick(btsl, btsr), pick(bwsl, bwsr)
    bn_abs = bn * sg
    root_s = pick(-ql, qr)
    inner = sm + bn_abs * pick(-iql, iqr)
    zero = jnp.zeros_like(sm)
    inner_pos = inner > 0.0
    lower_pos = lower > 0.0
    dbl = jnp.where(pos, jnp.where(lower_pos | inner_pos, zero, inner),
                    jnp.where(inner_pos, inner, zero))
    s = jnp.where(pos, jnp.where(lower_pos, zero, lower),
                  jnp.where(inner_pos | (upper > 0.0), upper, zero))

    ru = r * u
    energy = p * (1.0 / (GAMMA - 1.0)) + 0.5 * (ru * u + r * (t * t + w * w)) + (pt - p)
    vb = u * bn + t * bt + w * bw
    sb = sm * bn
    work = sb + ts * bts + ws * bws
    work2 = sb + t2 * bt2 + w2 * bw2
    energy_star = (rel * energy - pt * u + press_star * sm + bn * (vb - work)) * inv_dist
    dd = dbl * dens
    sd = s * dens
    sr = s * r
    f_r = ru + (sd - sr)
    f_n = ru * u + pt - bn2 + (sd * sm - sr * u)
    f_t = ru * t - bn * bt + (sd * ts - sr * t) + dd * (t2 - ts)
    f_w = ru * w - bn * bw + (sd * ws - sr * w) + dd * (w2 - ws)
    f_e = ((energy + pt) * u - bn * vb + s * (energy_star - energy)
           + dbl * (root_s * sg * (work - work2)))
    f_bt = bt * u - bn * t + s * (bts - bt) + dbl * (bt2 - bts)
    f_bw = bw * u - bn * w + s * (bws - bw) + dbl * (bw2 - bws)
    return (f_r, f_n, f_t, f_w, f_e, f_bt, f_bw)


def order_of(normal):
    n = normal
    t = n % 3 + 1
    w = t % 3 + 1
    return (0, n, t, w, 4, n + 4, t + 4, w + 4)


def flux_slots(normal):
    o = order_of(normal)
    return (o[0], o[1], o[2], o[3], o[4], o[6], o[7])


def params(mib):
    return pltpu.CompilerParams(vmem_limit_bytes=mib * MIB)


def pack(fields):
    def kernel(fields_ref, units_ref, stage_ref, in_sems, out_sems):
        arriving = []
        for u, pair in enumerate(PAIRS):
            copy = pltpu.make_async_copy(
                fields_ref.at[:, pl.ds(2 * pair, 2)], stage_ref.at[u], in_sems.at[u])
            copy.start()
            arriving.append(copy)
        leaving = []
        for u, pair in enumerate(PAIRS):
            arriving[u].wait()
            for f in range(FIELDS):
                h = (2 * pair + 2 * f) % HOLDERS
                copy = pltpu.make_async_copy(
                    stage_ref.at[u, f], units_ref.at[pl.ds(h, 2), u],
                    out_sems.at[u * FIELDS + f])
                copy.start()
                leaving.append(copy)
        for copy in leaving:
            copy.wait()

    return pl.pallas_call(
        kernel,
        out_shape=jax.ShapeDtypeStruct((HOLDERS, UNITS, CELLS, DEPTH), jnp.float32),
        in_specs=[HBM],
        out_specs=HBM,
        scratch_shapes=[
            pltpu.VMEM((UNITS, FIELDS, 2, CELLS, DEPTH), jnp.float32),
            pltpu.SemaphoreType.DMA((UNITS,)),
            pltpu.SemaphoreType.DMA((UNITS * FIELDS,)),
        ],
        name="pack",
    )(fields)


def rotate_rings(pos, offsets, shift, rings, peak):
    blocks = RING // CELLS

    def kernel(pos_ref, offsets_ref, shift_ref, peak_ref, ring_ref, out_ref, wide_ref):
        parity = pos_ref[0] & 1
        group = pos_ref[1]
        shear = shift_ref[0]

        def send(unit, slot, amount):
            for b in range(blocks):
                wide_ref[slot, b * CELLS:(b + 1) * CELLS, :] = ring_ref[b, unit]
            wide_ref[slot, RING:RING + CELLS, :] = ring_ref[0, unit]
            wide_ref[slot, RING + CELLS:, :] = ring_ref[1, unit, 0:8]
            low = (-amount) & 7
            for b in range(blocks):
                base = pl.multiple_of(((b * CELLS - amount) & (RING - 1)) - low, 8)
                block = wide_ref[slot, pl.ds(base, CELLS + 8), :]
                block = pltpu.roll(block, CELLS + 8 - low, 0)
                out_ref[b, slot * CELLS:(slot + 1) * CELLS, :] = block[0:CELLS]

        def amount_of(row):
            return offsets_ref[group * ROWS + row]

        for unit, pair in enumerate(PAIRS):
            send(unit, unit, amount_of(2 * pair + parity))
        last = group == GROUPS - 1
        row = jnp.where(last, ROWS - 2, 0) + parity
        send(jnp.where(last, 1, 0), UNITS, amount_of(row) + jnp.where(last, shear, -shear))
        for b in range(blocks):
            out_ref[b, PEAK:, :] = peak_ref[...]

    return pl.pallas_call(
        kernel,
        out_shape=jax.ShapeDtypeStruct((blocks, LINES, DEPTH), jnp.float32),
        in_specs=[SMEM, SMEM, SMEM, VMEM, VMEM],
        out_specs=VMEM,
        scratch_shapes=[pltpu.VMEM((UNITS + 1, RING + CELLS + 8, DEPTH), jnp.float32)],
        compiler_params=params(16),
        name="rotate",
    )(pos, offsets, shift, peak, rings)


def rims(pos, blocks):
    ghost = jax.ShapeDtypeStruct((FIELDS, 2, CELLS, DEPTH), jnp.float32)
    edge = jax.ShapeDtypeStruct((FIELDS, ROWS, 2, DEPTH), jnp.float32)

    def kernel(pos_ref, blocks_ref, left_ref, right_ref, up_ref, down_ref):
        group = pos_ref[1]
        top_at = pl.multiple_of(jnp.where(group == GROUPS - 1, EXTRA, CELLS), 8)
        low_at = pl.multiple_of(jnp.where(group == 0, EXTRA, 0), 8)
        for f in range(FIELDS):
            for u, pair in enumerate(PAIRS):
                for r in range(2):
                    h = (2 * pair + r + 2 * f) % HOLDERS
                    right_ref[f, 2 * pair + r] = blocks_ref[
                        h, (u + 1) * CELLS - 2:(u + 1) * CELLS, :]
                    left_ref[f, 2 * pair + r] = blocks_ref[h, u * CELLS:u * CELLS + 2, :]
            for r in range(2):
                top = (ROWS - 2 + r + 2 * f) % HOLDERS
                low = (r + 2 * f) % HOLDERS
                up_ref[f, r] = blocks_ref[top, pl.ds(top_at, CELLS), :]
                down_ref[f, r] = blocks_ref[low, pl.ds(low_at, CELLS), :]

    return pl.pallas_call(
        kernel,
        out_shape=(edge, edge, ghost, ghost),
        in_specs=[SMEM, VMEM],
        out_specs=(VMEM,) * 4,
        compiler_params=params(8),
        name="rims",
    )(pos, blocks)


PAD = 8
WIDE = 48
Z_BLOCK = 32
Z_UNROLL = 4
S_UNROLL = 2
R_BLOCK = 16
A_BLOCK = 16


def unit_of(row):
    pair = row >> 1
    return jnp.where(pair < 4, 2 * pair, 15 - 2 * pair)


def load(blocks_ref, row, start, size):
    at = pl.multiple_of(unit_of(row) * CELLS + start, 8)
    return [blocks_ref[(row + 2 * f) & (HOLDERS - 1), pl.ds(at, size), :]
            for f in range(FIELDS)]


def vertical(blocks, first, rows):
    order = order_of(3)
    slots = flux_slots(3)
    parts = CELLS // Z_BLOCK

    def kernel(blocks_ref, acc_ref, left_ref, right_ref, flux_ref):
        def states(r, carry):
            prim = to_primitive(load(blocks_ref, first + r, 0, CELLS))
            for k, f in enumerate(order):
                value = prim[f]
                below = pltpu.roll(value, 1, 1)
                above = pltpu.roll(value, DEPTH - 1, 1)
                beyond = pltpu.roll(value, DEPTH - 2, 1)
                step = above - value
                left_ref[k, r] = value + half_slope(value - below, step)
                right_ref[k, r] = above - half_slope(step, beyond - above)
            return carry

        lax.fori_loop(0, rows, states, 0, unroll=S_UNROLL)

        def fluxes(n, carry):
            r = n // parts if parts > 1 else n
            at = pl.ds(pl.multiple_of((n % parts if parts > 1 else 0) * Z_BLOCK, 8), Z_BLOCK)
            flux = hlld([left_ref[k, r, at, :] for k in range(8)],
                        [right_ref[k, r, at, :] for k in range(8)])
            for k in range(7):
                flux_ref[k, r, at, :] = flux[k]
            return carry

        lax.fori_loop(0, rows * parts, fluxes, 0)

        def changes(r, carry):
            state = load(blocks_ref, first + r, 0, CELLS)
            gains = [
                None,
                2.0 * OMEGA * state[2],
                -(2.0 - SHEAR) * OMEGA * state[1],
                None,
                SHEAR * OMEGA * (state[1] * state[2] / state[0] - state[5] * state[6]),
                None,
                -SHEAR * OMEGA * state[5],
                None,
            ]
            for k, slot in enumerate(slots):
                value = flux_ref[k, r]
                change = pltpu.roll(value, 1, 1) - value
                if gains[slot] is not None:
                    change = change + gains[slot]
                acc_ref[slot, r] = change
            return carry

        lax.fori_loop(0, rows, changes, 0, unroll=Z_UNROLL)

    sides = pltpu.VMEM((8, rows, CELLS, DEPTH), jnp.float32)
    return pl.pallas_call(
        kernel,
        out_shape=jax.ShapeDtypeStruct((FIELDS - 1, rows, CELLS, DEPTH), jnp.float32),
        in_specs=[VMEM],
        out_specs=VMEM,
        scratch_shapes=[sides, sides, sides],
        compiler_params=params(16),
        name=f"vertical{first}",
    )(blocks)


def march(order, window, runs):
    def face(at, steps, lefts):
        new_steps, new_lefts, rights = [], [], []
        here, there = window(at), window(at + 1)
        for k, f in enumerate(order):
            step = there[f] - here[f]
            slope = half_slope(steps[k], step)
            rights.append(here[f] - slope)
            new_lefts.append(here[f] + slope)
            new_steps.append(step)
        return hlld(lefts, rights), new_steps, new_lefts

    a, b, c = window(-2), window(-1), window(0)
    steps = [c[f] - b[f] for f in order]
    lefts = [b[f] + half_slope(b[f] - a[f], step) for f, step in zip(order, steps)]
    lower, steps, lefts = face(0, steps, lefts)

    def body(emit, i, carry):
        lower, steps, lefts = carry
        upper, steps, lefts = face(i + 1, steps, lefts)
        emit(i, lower, upper)
        return (upper, steps, lefts)

    carry = (lower, steps, lefts)
    for start, stop, emit in runs:
        carry = lax.fori_loop(start, stop, functools.partial(body, emit), carry)


def finish(blocks, accs, below, above, before, after):
    def kernel(blocks_ref, acc0_ref, acc1_ref, below_ref, above_ref, before_ref, after_ref,
               out_ref, prim_ref, turn_ref):
        def put(values, row, start, size):
            for f in range(FIELDS):
                prim_ref[f, pl.ds(pl.multiple_of(row * WIDE, 8) + start, size), :] = values[f]

        def fill(i, carry):
            put(to_primitive(load(blocks_ref, i, 0, CELLS)), i + 2, PAD, CELLS)
            put(to_primitive([before_ref[f, i] for f in range(FIELDS)]), i + 2, PAD - 2, 2)
            put(to_primitive([after_ref[f, i] for f in range(FIELDS)]), i + 2, PAD + CELLS, 2)
            return carry

        lax.fori_loop(0, ROWS, fill, 0)
        for r in range(2):
            put(to_primitive([below_ref[f, r] for f in range(FIELDS)]), r, PAD, CELLS)
            put(to_primitive([above_ref[f, r] for f in range(FIELDS)]), ROWS + 2 + r, PAD, CELLS)

        for start in range(0, ROWS, A_BLOCK):
            def rows_at(a):
                return [jnp.concatenate([
                    prim_ref[f, pl.ds((start + g + 2) * WIDE + PAD + a, 8, stride=WIDE), :]
                    for g in range(0, A_BLOCK, 8)], axis=0) for f in range(FIELDS)]

            def keep(a, lower, upper):
                at = pl.ds(pl.multiple_of(a * ROWS, 8) + start, A_BLOCK)
                for k in range(7):
                    turn_ref[k, at, :] = lower[k] - upper[k]

            march(order_of(2), rows_at, [(0, CELLS, keep)])

        a_slots = flux_slots(2)
        slots = flux_slots(1)
        peak = blocks_ref[0, PEAK:, :]
        for b in range(1, HOLDERS):
            peak = jnp.maximum(peak, blocks_ref[b, PEAK:, :])
        dt = CFL_NUMBER / peak[0:1]

        for start in range(0, CELLS, R_BLOCK):
            part = slice(start, start + R_BLOCK)

            def cells_at(i):
                at = pl.multiple_of((i + 2) * WIDE, 8) + PAD + start
                return [prim_ref[f, pl.ds(at, R_BLOCK), :] for f in range(FIELDS)]

            def update(acc_ref, first, i, lower, upper):
                state = load(blocks_ref, i, start, R_BLOCK)
                change = [None] * FIELDS
                for k, slot in enumerate(slots):
                    change[slot] = lower[k] - upper[k]
                for k, slot in enumerate(a_slots):
                    turn = jnp.concatenate([
                        turn_ref[k, pl.ds((start + g) * ROWS + i, 8, stride=ROWS), :]
                        for g in range(0, R_BLOCK, 8)], axis=0)
                    change[slot] = turn if change[slot] is None else change[slot] + turn
                for slot in range(FIELDS - 1):
                    total = acc_ref[slot, i - first, part, :]
                    total = total if change[slot] is None else total + change[slot]
                    out_ref[slot, i, part, :] = state[slot] + dt * total
                out_ref[7, i, part, :] = state[7] + dt * change[7]

            half = ROWS // 2
            march(order_of(1), cells_at, [
                (0, half, functools.partial(update, acc0_ref, 0)),
                (half, ROWS, functools.partial(update, acc1_ref, half))])

    return pl.pallas_call(
        kernel,
        out_shape=jax.ShapeDtypeStruct((FIELDS, ROWS, CELLS, DEPTH), jnp.float32),
        in_specs=[VMEM] * 7,
        out_specs=VMEM,
        scratch_shapes=[
            pltpu.VMEM((FIELDS, (ROWS + 4) * WIDE, DEPTH), jnp.float32),
            pltpu.VMEM((7, CELLS * ROWS, DEPTH), jnp.float32),
        ],
        compiler_params=params(24),
        name="finish",
    )(blocks, *accs, below, above, before, after)


def over(peak, axis):
    for by in (1, 2, 4, 8):
        peak = jnp.maximum(peak, passed_along(peak, axis, by))
    return peak


def exchanged(units):
    return lax.all_to_all(units, AZ, split_axis=0, concat_axis=0, tiled=True)


def local(fields, offsets, boundary_shift):
    pos = jnp.stack([lax.axis_index(AZ), lax.axis_index(RAD)]).astype(jnp.int32)
    rings = exchanged(pack(fields))
    peak = jnp.broadcast_to(jnp.max(cell_speed(to_primitive(fields))), (8, DEPTH))
    peak = over(peak, RAD)
    blocks = exchanged(rotate_rings(pos, offsets, boundary_shift, rings, peak))
    left, right, up, down = rims(pos, blocks)
    acc0 = vertical(blocks, 0, ROWS // 2)
    acc0, left, right, up, down = lax.optimization_barrier((acc0, left, right, up, down))
    below = passed_along(up, RAD, 1)
    above = passed_along(down, RAD, -1)
    before = passed_along(right, AZ, 1)
    after = passed_along(left, AZ, -1)
    acc1 = vertical(blocks, ROWS // 2, ROWS // 2)
    return finish(blocks, (acc0, acc1), below, above, before, after)


def solution(mesh):
    split = Mesh(mesh.devices.reshape(8, 2, 4, 2, 2), ("az_0", "az_1", "rad_0", "rad_1", "rad_2"))
    return jax.shard_map(
        local,
        mesh=split,
        in_specs=(P(None, RAD, AZ, None), P(), P()),
        out_specs=P(None, RAD, AZ, None),
        check_vma=False,
    )
```

```python
import functools

import jax
import jax.numpy as jnp
from jax import lax
from jax.experimental import pallas as pl
from jax.experimental.pallas import tpu as pltpu
from jax.sharding import PartitionSpec as P


AZ = "az"
RAD = "rad"

GAMMA = 5.0 / 3.0
CFL_NUMBER = 0.4
OMEGA = 1.0
SHEAR = 1.5

FIELDS = 8
ROWS = 16
CELLS = 32
RING = 512
DEPTH = 128
GROUPS = 16
HOLDERS = 16
UNITS = 8
PAIRS = (0, 7, 1, 6, 2, 5, 3, 4)
EXTRA = UNITS * CELLS
LINES = EXTRA + CELLS
GHOSTS = FIELDS * 2 * CELLS
ORDER = tuple(2 * z + x for x in (0, 1) for z in (0, 7, 1, 6, 2, 5, 3, 4))
BACK = ORDER[::-1]
PLACE = tuple(ORDER.index(d) for d in range(HOLDERS))
HOLDER = tuple(BACK.index(d) for d in range(HOLDERS))
TINY = 1e-30
VMEM = pl.BlockSpec(memory_space=pltpu.VMEM)
SMEM = pl.BlockSpec(memory_space=pltpu.SMEM)
HBM = pl.BlockSpec(memory_space=pl.ANY)
MIB = 1024 * 1024


def passed_along(array, axis, by):
    devices = lax.axis_size(axis)
    return lax.ppermute(array, axis, [(i, (i + by) % devices) for i in range(devices)])


def to_primitive(state):
    density = state[0]
    inverse = 1.0 / density
    vx = state[1] * inverse
    vy = state[2] * inverse
    vz = state[3] * inverse
    kinetic = 0.5 * (state[1] * vx + state[2] * vy + state[3] * vz)
    magnetic = 0.5 * (state[5] * state[5] + state[6] * state[6] + state[7] * state[7])
    pressure = (GAMMA - 1.0) * (state[4] - kinetic - magnetic)
    return (density, vx, vy, vz, pressure, state[5], state[6], state[7])


def fast_speed(density, pressure, normal_field, field_sq):
    sound = (GAMMA * pressure + field_sq) / density
    spread = jnp.maximum(
        sound * sound
        - 4.0 * GAMMA * pressure * normal_field * normal_field / (density * density),
        0.0,
    )
    return jnp.sqrt(0.5 * (sound + jnp.sqrt(spread)))


def cell_speed(prim):
    field_sq = prim[5] * prim[5] + prim[6] * prim[6] + prim[7] * prim[7]
    total = jnp.abs(prim[1]) + fast_speed(prim[0], prim[4], prim[5], field_sq)
    total = total + jnp.abs(prim[2]) + fast_speed(prim[0], prim[4], prim[6], field_sq)
    return total + jnp.abs(prim[3]) + fast_speed(prim[0], prim[4], prim[7], field_sq)


def half_slope(before, after):
    return 0.5 * jnp.minimum(
        jnp.maximum(after, jnp.minimum(before, 0.0)), jnp.maximum(before, 0.0)
    )


def hlld(left, right):
    rl, ul, tl, wl, pl_, nl, btl, bwl = left
    rr, ur, tr, wr, pr_, nr, btr, bwr = right
    bn = 0.5 * (nl + nr)
    bn2 = bn * bn
    bn2_4 = (4.0 * GAMMA) * bn2

    def signal(r, p, bt, bw):
        b2 = bn2 + (bt * bt + bw * bw)
        h = GAMMA * p + b2
        square = jnp.maximum(h * h - p * bn2_4, TINY)
        return (h + square * lax.rsqrt(square)) * (1.0 / r), p + 0.5 * b2

    sig_l, ptl = signal(rl, pl_, btl, bwl)
    sig_r, ptr = signal(rr, pr_, btr, bwr)
    square = 0.5 * jnp.maximum(sig_l, sig_r)
    fastest = square * lax.rsqrt(square)
    lower = jnp.minimum(ul, ur) - fastest
    upper = jnp.maximum(ul, ur) + fastest
    rel_l = lower - ul
    rel_r = upper - ur
    ml = rl * rel_l
    mr = rr * rel_r
    guess = (mr * ur - ml * ul - ptr + ptl) * (1.0 / (mr - ml))
    margin = 0.1 * (upper - lower)
    sm = jnp.minimum(jnp.maximum(guess, lower + margin), upper - margin)
    press_star = ptl + ml * (sm - ul)

    def star(m, rel, outer, u, t, w, bt, bw):
        dist = outer - sm
        product = m * dist
        inv_div = 1.0 / jnp.maximum(product - bn2, 0.5 * product)
        k = (sm - u) * (bn * inv_div)
        factor = (m * rel - bn2) * inv_div
        dens = m * (1.0 / dist)
        return (dens, dens * lax.rsqrt(dens),
                t - bt * k, w - bw * k, bt * factor, bw * factor)

    dl, ql, tsl, wsl, btsl, bwsl = star(ml, rel_l, lower, ul, tl, wl, btl, bwl)
    dr, qr, tsr, wsr, btsr, bwsr = star(mr, rel_r, upper, ur, tr, wr, btr, bwr)
    inv_sum = 1.0 / (ql + qr)
    al = ql * inv_sum
    ar = qr * inv_sum

    pos = sm > 0.0

    def pick(a, b):
        return jnp.where(pos, a, b)

    sg = jnp.where(bn < 0.0, -1.0, 1.0)
    sgs = sg * inv_sum
    qqs = (ql * qr) * sgs
    side_sg = pick(-sg, sg)
    own, other = pick(ar, -al), pick(al, -ar)
    jump_t, jump_w = tsr - tsl, wsr - wsl
    jump_bt, jump_bw = btsr - btsl, bwsr - bwsl
    more_t = own * jump_t + sgs * jump_bt
    more_w = own * jump_w + sgs * jump_bw
    more_bt = other * jump_bt + qqs * jump_t
    more_bw = other * jump_bw + qqs * jump_w

    r, u, t, w, p = pick(rl, rr), pick(ul, ur), pick(tl, tr), pick(wl, wr), pick(pl_, pr_)
    bt, bw, pt, outer = pick(btl, btr), pick(bwl, bwr), pick(ptl, ptr), pick(lower, upper)
    dens = pick(dl, dr)
    ts, ws, bts, bws = pick(tsl, tsr), pick(wsl, wsr), pick(btsl, btsr), pick(bwsl, bwsr)
    inv_root = lax.rsqrt(dens)
    inner = sm + (bn * side_sg) * inv_root
    inside = jnp.logical_not(lower > 0.0)
    inner_pos = inner > 0.0
    s = jnp.where(inside & (inner_pos | (upper > 0.0)), outer, 0.0)
    dbl = jnp.where(inside & (inner_pos ^ pos), inner, 0.0)

    energy = pt + 0.5 * (p + r * (u * u + t * t + w * w))
    vb = u * bn + t * bt + w * bw
    work = sm * bn + ts * bts + ws * bws
    more_work = (ts * more_bt + more_t * (bts + more_bt)
                 + ws * more_bw + more_w * (bws + more_bw))
    ptu = pt * u
    energy_star = ((outer - u) * energy - ptu + press_star * sm + bn * (vb - work)) * (
        1.0 / (outer - sm))
    us = u - s
    mm = r * us
    sd = s * dens
    dd = dbl * dens
    f_r = mm + sd
    f_n = mm * u + sd * sm + (pt - bn2)
    f_t = mm * t + sd * ts - bn * bt + dd * more_t
    f_w = mm * w + sd * ws - bn * bw + dd * more_w
    f_e = (energy * us + ptu - bn * vb + s * energy_star
           - dbl * ((dens * inv_root) * side_sg * more_work))
    f_bt = bt * us - bn * t + s * bts + dbl * more_bt
    f_bw = bw * us - bn * w + s * bws + dbl * more_bw
    return (f_r, f_n, f_t, f_w, f_e, f_bt, f_bw)


def order_of(normal):
    n = normal
    t = n % 3 + 1
    w = t % 3 + 1
    return (0, n, t, w, 4, n + 4, t + 4, w + 4)


def flux_slots(normal):
    o = order_of(normal)
    return (o[0], o[1], o[2], o[3], o[4], o[6], o[7])


def params(mib):
    return pltpu.CompilerParams(vmem_limit_bytes=mib * MIB)


def pack(fields):
    def kernel(fields_ref, units_ref, stage_ref, in_sems, out_sems):
        arriving = []
        for u, pair in enumerate(PAIRS):
            copy = pltpu.make_async_copy(
                fields_ref.at[:, pl.ds(2 * pair, 2)], stage_ref.at[u], in_sems.at[u])
            copy.start()
            arriving.append(copy)
        leaving = []
        for u, pair in enumerate(PAIRS):
            arriving[u].wait()
            for f in range(FIELDS):
                for r in range(2):
                    place = PLACE[BACK[(2 * pair + r + 2 * f) % HOLDERS]]
                    copy = pltpu.make_async_copy(
                        stage_ref.at[u, f, r], units_ref.at[place, u],
                        out_sems.at[(u * FIELDS + f) * 2 + r])
                    copy.start()
                    leaving.append(copy)
        for copy in leaving:
            copy.wait()

    return pl.pallas_call(
        kernel,
        out_shape=jax.ShapeDtypeStruct((HOLDERS, UNITS, CELLS, DEPTH), jnp.float32),
        in_specs=[HBM],
        out_specs=HBM,
        scratch_shapes=[
            pltpu.VMEM((UNITS, FIELDS, 2, CELLS, DEPTH), jnp.float32),
            pltpu.SemaphoreType.DMA((UNITS,)),
            pltpu.SemaphoreType.DMA((UNITS * FIELDS * 2,)),
        ],
        name="pack",
    )(fields)


def rotate_rings(pos, offsets, shift, rings, peak):
    blocks = RING // CELLS

    def kernel(pos_ref, offsets_ref, shift_ref, peak_ref, ring_ref, out_ref, wide_ref):
        parity = pos_ref[0] & 1
        group = pos_ref[1]
        shear = shift_ref[0]

        def send(unit, slot, amount):
            for b in range(blocks):
                wide_ref[slot, b * CELLS:(b + 1) * CELLS, :] = ring_ref[PLACE[b], unit]
            wide_ref[slot, RING:RING + CELLS, :] = ring_ref[PLACE[0], unit]
            wide_ref[slot, RING + CELLS:, :] = ring_ref[PLACE[1], unit, 0:8]
            low = (-amount) & 7
            for b in range(blocks):
                base = pl.multiple_of(((b * CELLS - amount) & (RING - 1)) - low, 8)
                block = wide_ref[slot, pl.ds(base, CELLS + 8), :]
                block = pltpu.roll(block, CELLS + 8 - low, 0)
                out_ref[HOLDER[b], slot * CELLS:(slot + 1) * CELLS, :] = block[0:CELLS]

        def amount_of(row):
            return offsets_ref[group * ROWS + row]

        for unit, pair in enumerate(PAIRS):
            send(unit, unit, amount_of(2 * pair + parity))
        last = group == GROUPS - 1
        row = jnp.where(last, ROWS - 2, 0) + parity
        send(jnp.where(last, 1, 0), UNITS, amount_of(row) + jnp.where(last, shear, -shear))

        @pl.when((group > 0) & (group < GROUPS - 1))
        def _():
            for b in range(blocks):
                out_ref[b, EXTRA:EXTRA + 8, :] = peak_ref[...]

    return pl.pallas_call(
        kernel,
        out_shape=jax.ShapeDtypeStruct((blocks, LINES, DEPTH), jnp.float32),
        in_specs=[SMEM, SMEM, SMEM, VMEM, VMEM],
        out_specs=VMEM,
        scratch_shapes=[pltpu.VMEM((UNITS + 1, RING + CELLS + 8, DEPTH), jnp.float32)],
        compiler_params=params(16),
        name="rotate",
    )(pos, offsets, shift, peak, rings)


def peak_of(blocks_ref):
    peak = blocks_ref[0, EXTRA:EXTRA + 8, :]
    for h in range(1, HOLDERS):
        peak = jnp.maximum(peak, blocks_ref[h, EXTRA:EXTRA + 8, :])
    return peak


def rims(pos, blocks):
    ghost = jax.ShapeDtypeStruct((GHOSTS + 8, DEPTH), jnp.float32)
    edge = jax.ShapeDtypeStruct((FIELDS, ROWS, 2, DEPTH), jnp.float32)

    def kernel(pos_ref, blocks_ref, left_ref, right_ref, up_ref, down_ref):
        group = pos_ref[1]
        top_at = pl.multiple_of(jnp.where(group == GROUPS - 1, EXTRA, CELLS), 8)
        low_at = pl.multiple_of(jnp.where(group == 0, EXTRA, 0), 8)
        for f in range(FIELDS):
            for u, pair in enumerate(PAIRS):
                for r in range(2):
                    h = (2 * pair + r + 2 * f) % HOLDERS
                    right_ref[f, 2 * pair + r] = blocks_ref[
                        h, (u + 1) * CELLS - 2:(u + 1) * CELLS, :]
                    left_ref[f, 2 * pair + r] = blocks_ref[h, u * CELLS:u * CELLS + 2, :]
            for r in range(2):
                top = (ROWS - 2 + r + 2 * f) % HOLDERS
                low = (r + 2 * f) % HOLDERS
                at = (2 * f + r) * CELLS
                up_ref[at:at + CELLS, :] = blocks_ref[top, pl.ds(top_at, CELLS), :]
                down_ref[at:at + CELLS, :] = blocks_ref[low, pl.ds(low_at, CELLS), :]
        peak = peak_of(blocks_ref)
        up_ref[GHOSTS:, :] = peak
        down_ref[GHOSTS:, :] = peak

    return pl.pallas_call(
        kernel,
        out_shape=(edge, edge, ghost, ghost),
        in_specs=[SMEM, VMEM],
        out_specs=(VMEM,) * 4,
        compiler_params=params(8),
        name="rims",
    )(pos, blocks)


PAD = 8
WIDE = 48
R_BLOCK = CELLS // 2


def unit_of(row):
    pair = row >> 1
    return jnp.where(pair < 4, 2 * pair, 15 - 2 * pair)


def load(blocks_ref, row, start, size):
    at = pl.multiple_of(unit_of(row) * CELLS + start, 8)
    return [blocks_ref[(row + 2 * f) & (HOLDERS - 1), pl.ds(at, size), :]
            for f in range(FIELDS)]


def vertical(blocks, first, rows):
    order = order_of(3)
    slots = flux_slots(3)

    def kernel(blocks_ref, acc_ref, left_ref, right_ref, flux_ref):
        def states(r):
            prim = to_primitive(load(blocks_ref, first + r, 0, CELLS))
            for k, f in enumerate(order):
                value = prim[f]
                below = pltpu.roll(value, 1, 1)
                above = pltpu.roll(value, DEPTH - 1, 1)
                beyond = pltpu.roll(value, DEPTH - 2, 1)
                step = above - value
                left_ref[k, r] = value + half_slope(value - below, step)
                right_ref[k, r] = above - half_slope(step, beyond - above)

        def fluxes(r):
            flux = hlld([left_ref[k, r] for k in range(8)], [right_ref[k, r] for k in range(8)])
            for k in range(7):
                flux_ref[k, r] = flux[k]

        def changes(r):
            state = load(blocks_ref, first + r, 0, CELLS)
            gains = [
                None,
                2.0 * OMEGA * state[2],
                -(2.0 - SHEAR) * OMEGA * state[1],
                None,
                SHEAR * OMEGA * (state[1] * state[2] / state[0] - state[5] * state[6]),
                None,
                -SHEAR * OMEGA * state[5],
                None,
            ]
            for k, slot in enumerate(slots):
                value = flux_ref[k, r]
                change = pltpu.roll(value, 1, 1) - value
                if gains[slot] is not None:
                    change = change + gains[slot]
                acc_ref[slot, r] = change

        states(0)

        def body(r, carry):
            changes(jnp.maximum(r - 1, 0))
            fluxes(r)
            states(jnp.minimum(r + 1, rows - 1))
            return carry

        lax.fori_loop(0, rows, body, 0)
        changes(rows - 1)

    sides = pltpu.VMEM((8, rows, CELLS, DEPTH), jnp.float32)
    return pl.pallas_call(
        kernel,
        out_shape=jax.ShapeDtypeStruct((FIELDS - 1, rows, CELLS, DEPTH), jnp.float32),
        in_specs=[VMEM],
        out_specs=VMEM,
        scratch_shapes=[sides, sides, sides],
        compiler_params=params(16),
    )(blocks)


def march(order, window, runs):
    def face(at, steps, lefts):
        new_steps, new_lefts, rights = [], [], []
        here, there = window(at), window(at + 1)
        for k, f in enumerate(order):
            step = there[f] - here[f]
            slope = half_slope(steps[k], step)
            rights.append(here[f] - slope)
            new_lefts.append(here[f] + slope)
            new_steps.append(step)
        return hlld(lefts, rights), new_steps, new_lefts

    a, b, c = window(-2), window(-1), window(0)
    steps = [c[f] - b[f] for f in order]
    lefts = [b[f] + half_slope(b[f] - a[f], step) for f, step in zip(order, steps)]
    lower, steps, lefts = face(0, steps, lefts)

    def body(emit, i, carry):
        lower, steps, lefts = carry
        upper, steps, lefts = face(i + 1, steps, lefts)
        emit(i, lower, upper)
        return (upper, steps, lefts)

    carry = (lower, steps, lefts)
    for start, stop, emit in runs:
        carry = lax.fori_loop(start, stop, functools.partial(body, emit), carry)


def fill(blocks_ref, prim_ref, top, start, size):
    def body(i, carry):
        values = to_primitive(load(blocks_ref, i, start, size))
        at = pl.multiple_of((i + top) * WIDE, 8) + PAD + start
        for f in range(FIELDS):
            prim_ref[f, pl.ds(at, size), :] = values[f]
        return carry

    lax.fori_loop(0, ROWS, body, 0)


def azimuthal(blocks, edge, half):
    first = half * (CELLS // 2)

    def kernel(blocks_ref, edge_ref, turn_ref, prim_ref):
        fill(blocks_ref, prim_ref, 0, 8 * half, CELLS - 8)
        at = PAD + CELLS if half else PAD - 2

        def sides(i, carry):
            values = to_primitive([edge_ref[f, i] for f in range(FIELDS)])
            for f in range(FIELDS):
                prim_ref[f, pl.ds(pl.multiple_of(i * WIDE, 8) + at, 2), :] = values[f]
            return carry

        lax.fori_loop(0, ROWS, sides, 0, unroll=4)

        def rows_at(a):
            return [jnp.concatenate([
                prim_ref[f, pl.ds(g * WIDE + PAD + first + a, 8, stride=WIDE), :]
                for g in range(0, ROWS, 8)], axis=0) for f in range(FIELDS)]

        def keep(a, lower, upper):
            for k in range(7):
                turn_ref[k, pl.ds(pl.multiple_of(a * ROWS, 8), ROWS), :] = lower[k] - upper[k]

        march(order_of(2), rows_at, [(0, CELLS // 2, keep)])

    return pl.pallas_call(
        kernel,
        out_shape=jax.ShapeDtypeStruct((7, CELLS // 2 * ROWS, DEPTH), jnp.float32),
        in_specs=[VMEM] * 2,
        out_specs=VMEM,
        scratch_shapes=[pltpu.VMEM((FIELDS, ROWS * WIDE, DEPTH), jnp.float32)],
        compiler_params=params(12),
    )(blocks, edge)


def finish(pos, blocks, accs, turns, below, above):
    def kernel(pos_ref, blocks_ref, acc0_ref, acc1_ref, turn0_ref, turn1_ref, below_ref, above_ref,
               out_ref, prim_ref):
        fill(blocks_ref, prim_ref, 2, 0, CELLS)
        for ghost_ref, row in ((below_ref, 0), (above_ref, ROWS + 2)):
            for r in range(2):
                values = to_primitive([
                    ghost_ref[(2 * f + r) * CELLS:(2 * f + r + 1) * CELLS, :]
                    for f in range(FIELDS)])
                at = (row + r) * WIDE + PAD
                for f in range(FIELDS):
                    prim_ref[f, at:at + CELLS, :] = values[f]

        a_slots = flux_slots(2)
        slots = flux_slots(1)
        group = pos_ref[1]
        peak = jnp.where(
            group == 0, above_ref[GHOSTS:, :],
            jnp.where(group == GROUPS - 1, below_ref[GHOSTS:, :], peak_of(blocks_ref)))
        dt = CFL_NUMBER / peak[0:1]

        for start, turn_ref in ((0, turn0_ref), (R_BLOCK, turn1_ref)):
            part = slice(start, start + R_BLOCK)

            def cells_at(i):
                at = pl.multiple_of((i + 2) * WIDE, 8) + PAD + start
                return [prim_ref[f, pl.ds(at, R_BLOCK), :] for f in range(FIELDS)]

            def update(acc_ref, first, i, lower, upper):
                state = load(blocks_ref, i, start, R_BLOCK)
                change = [None] * FIELDS
                for k, slot in enumerate(slots):
                    change[slot] = lower[k] - upper[k]
                for k, slot in enumerate(a_slots):
                    turn = jnp.concatenate([
                        turn_ref[k, pl.ds(g * ROWS + i, 8, stride=ROWS), :]
                        for g in range(0, R_BLOCK, 8)], axis=0)
                    change[slot] = turn if change[slot] is None else change[slot] + turn
                for slot in range(FIELDS - 1):
                    total = acc_ref[slot, i - first, part, :]
                    total = total if change[slot] is None else total + change[slot]
                    out_ref[slot, i, part, :] = state[slot] + dt * total
                out_ref[7, i, part, :] = state[7] + dt * change[7]

            half = ROWS // 2
            march(order_of(1), cells_at, [
                (0, half, functools.partial(update, acc0_ref, 0)),
                (half, ROWS, functools.partial(update, acc1_ref, half))])

    return pl.pallas_call(
        kernel,
        out_shape=jax.ShapeDtypeStruct((FIELDS, ROWS, CELLS, DEPTH), jnp.float32),
        in_specs=[SMEM] + [VMEM] * 7,
        out_specs=VMEM,
        scratch_shapes=[pltpu.VMEM((FIELDS, (ROWS + 4) * WIDE, DEPTH), jnp.float32)],
        compiler_params=params(20),
        name="finish",
    )(pos, blocks, *accs, *turns, below, above)


def over(peak, axis):
    for by in (1, 2, 4, 8):
        peak = jnp.maximum(peak, passed_along(peak, axis, by))
    return peak


def exchanged(units, order):
    return lax.all_to_all(units, AZ, split_axis=0, concat_axis=0, tiled=True,
                          axis_index_groups=[list(order)])


def local(fields, offsets, boundary_shift):
    holder = jnp.take(jnp.array(HOLDER, jnp.int32), lax.axis_index(AZ))
    pos = jnp.stack([holder, lax.axis_index(RAD).astype(jnp.int32)])
    rings = exchanged(pack(fields), ORDER)
    peak = jnp.broadcast_to(jnp.max(cell_speed(to_primitive(fields))), (8, DEPTH))
    peak = over(peak, RAD)
    blocks = exchanged(rotate_rings(pos, offsets, boundary_shift, rings, peak), BACK)
    left, right, up, down = rims(pos, blocks)
    before = passed_along(right, AZ, 1)
    acc0 = vertical(blocks, 0, ROWS // 2)
    acc0, up, blocks = lax.optimization_barrier((acc0, up, blocks))
    below = passed_along(up, RAD, 1)
    acc1 = vertical(blocks, ROWS // 2, ROWS // 2)
    acc1, left, blocks = lax.optimization_barrier((acc1, left, blocks))
    after = passed_along(left, AZ, -1)
    turn0 = azimuthal(blocks, before, 0)
    turn0, down, blocks = lax.optimization_barrier((turn0, down, blocks))
    above = passed_along(down, RAD, -1)
    turn1 = azimuthal(blocks, after, 1)
    return finish(pos, blocks, (acc0, acc1), (turn0, turn1), below, above)


def solution(mesh):
    return jax.shard_map(
        local,
        mesh=mesh,
        in_specs=(P(None, RAD, AZ, None), P(), P()),
        out_specs=P(None, RAD, AZ, None),
        check_vma=False,
    )
```

```python
import functools

import jax
import jax.numpy as jnp
from jax import lax
from jax.experimental import pallas as pl
from jax.experimental.pallas import tpu as pltpu
from jax.sharding import PartitionSpec as P


AZ = "az"
RAD = "rad"

GAMMA = 5.0 / 3.0
CFL_NUMBER = 0.4
OMEGA = 1.0
SHEAR = 1.5

FIELDS = 8
ROWS = 16
CELLS = 32
RING = 512
DEPTH = 128
GROUPS = 16
HOLDERS = 16
UNITS = 8
PAIRS = (0, 7, 1, 6, 2, 5, 3, 4)
EXTRA = UNITS * CELLS
LINES = EXTRA + CELLS
GHOSTS = FIELDS * 2 * CELLS
ORDER = tuple(2 * z + x for x in (0, 1) for z in (0, 7, 1, 6, 2, 5, 3, 4))
BACK = ORDER[::-1]
PLACE = tuple(ORDER.index(d) for d in range(HOLDERS))
HOLDER = tuple(BACK.index(d) for d in range(HOLDERS))
TINY = 1e-30
VMEM = pl.BlockSpec(memory_space=pltpu.VMEM)
SMEM = pl.BlockSpec(memory_space=pltpu.SMEM)
HBM = pl.BlockSpec(memory_space=pl.ANY)
MIB = 1024 * 1024


def passed_along(array, axis, by):
    devices = lax.axis_size(axis)
    return lax.ppermute(array, axis, [(i, (i + by) % devices) for i in range(devices)])


def to_primitive(state):
    density = state[0]
    inverse = 1.0 / density
    vx = state[1] * inverse
    vy = state[2] * inverse
    vz = state[3] * inverse
    kinetic = 0.5 * (state[1] * vx + state[2] * vy + state[3] * vz)
    magnetic = 0.5 * (state[5] * state[5] + state[6] * state[6] + state[7] * state[7])
    pressure = (GAMMA - 1.0) * (state[4] - kinetic - magnetic)
    return (density, vx, vy, vz, pressure, state[5], state[6], state[7])


def fast_speed(density, pressure, normal_field, field_sq):
    sound = (GAMMA * pressure + field_sq) / density
    spread = jnp.maximum(
        sound * sound
        - 4.0 * GAMMA * pressure * normal_field * normal_field / (density * density),
        0.0,
    )
    return jnp.sqrt(0.5 * (sound + jnp.sqrt(spread)))


def cell_speed(prim):
    field_sq = prim[5] * prim[5] + prim[6] * prim[6] + prim[7] * prim[7]
    total = jnp.abs(prim[1]) + fast_speed(prim[0], prim[4], prim[5], field_sq)
    total = total + jnp.abs(prim[2]) + fast_speed(prim[0], prim[4], prim[6], field_sq)
    return total + jnp.abs(prim[3]) + fast_speed(prim[0], prim[4], prim[7], field_sq)


def half_slope(before, after):
    return 0.5 * jnp.minimum(
        jnp.maximum(after, jnp.minimum(before, 0.0)), jnp.maximum(before, 0.0)
    )


def hlld(left, right):
    rl, ul, tl, wl, pl_, nl, btl, bwl = left
    rr, ur, tr, wr, pr_, nr, btr, bwr = right
    bn = 0.5 * (nl + nr)
    bn2 = bn * bn
    bn2_4 = (4.0 * GAMMA) * bn2

    def signal(r, p, bt, bw):
        b2 = bn2 + (bt * bt + bw * bw)
        h = GAMMA * p + b2
        square = jnp.maximum(h * h - p * bn2_4, TINY)
        return (h + square * lax.rsqrt(square)) * (1.0 / r), p + 0.5 * b2

    sig_l, ptl = signal(rl, pl_, btl, bwl)
    sig_r, ptr = signal(rr, pr_, btr, bwr)
    square = 0.5 * jnp.maximum(sig_l, sig_r)
    fastest = square * lax.rsqrt(square)
    lower = jnp.minimum(ul, ur) - fastest
    upper = jnp.maximum(ul, ur) + fastest
    rel_l = lower - ul
    rel_r = upper - ur
    ml = rl * rel_l
    mr = rr * rel_r
    guess = (mr * ur - ml * ul - ptr + ptl) * (1.0 / (mr - ml))
    margin = 0.1 * (upper - lower)
    sm = jnp.minimum(jnp.maximum(guess, lower + margin), upper - margin)
    press_star = ptl + ml * (sm - ul)

    def star(m, rel, outer, u, t, w, bt, bw):
        dist = outer - sm
        product = m * dist
        inv_div = 1.0 / jnp.maximum(product - bn2, 0.5 * product)
        k = (sm - u) * (bn * inv_div)
        factor = (m * rel - bn2) * inv_div
        dens = m * (1.0 / dist)
        return (dens, dens * lax.rsqrt(dens),
                t - bt * k, w - bw * k, bt * factor, bw * factor)

    dl, ql, tsl, wsl, btsl, bwsl = star(ml, rel_l, lower, ul, tl, wl, btl, bwl)
    dr, qr, tsr, wsr, btsr, bwsr = star(mr, rel_r, upper, ur, tr, wr, btr, bwr)
    inv_sum = 1.0 / (ql + qr)
    al = ql * inv_sum
    ar = qr * inv_sum

    pos = sm > 0.0

    def pick(a, b):
        return jnp.where(pos, a, b)

    sg = jnp.where(bn < 0.0, -1.0, 1.0)
    sgs = sg * inv_sum
    qqs = (ql * qr) * sgs
    side_sg = pick(-sg, sg)
    own, other = pick(ar, -al), pick(al, -ar)
    jump_t, jump_w = tsr - tsl, wsr - wsl
    jump_bt, jump_bw = btsr - btsl, bwsr - bwsl
    more_t = own * jump_t + sgs * jump_bt
    more_w = own * jump_w + sgs * jump_bw
    more_bt = other * jump_bt + qqs * jump_t
    more_bw = other * jump_bw + qqs * jump_w

    r, u, t, w, p = pick(rl, rr), pick(ul, ur), pick(tl, tr), pick(wl, wr), pick(pl_, pr_)
    bt, bw, pt, outer = pick(btl, btr), pick(bwl, bwr), pick(ptl, ptr), pick(lower, upper)
    dens = pick(dl, dr)
    ts, ws, bts, bws = pick(tsl, tsr), pick(wsl, wsr), pick(btsl, btsr), pick(bwsl, bwsr)
    inv_root = lax.rsqrt(dens)
    inner = sm + (bn * side_sg) * inv_root
    inside = jnp.logical_not(lower > 0.0)
    inner_pos = inner > 0.0
    s = jnp.where(inside & (inner_pos | (upper > 0.0)), outer, 0.0)
    dbl = jnp.where(inside & (inner_pos ^ pos), inner, 0.0)

    energy = pt + 0.5 * (p + r * (u * u + t * t + w * w))
    vb = u * bn + t * bt + w * bw
    work = sm * bn + ts * bts + ws * bws
    more_work = (ts * more_bt + more_t * (bts + more_bt)
                 + ws * more_bw + more_w * (bws + more_bw))
    ptu = pt * u
    energy_star = ((outer - u) * energy - ptu + press_star * sm + bn * (vb - work)) * (
        1.0 / (outer - sm))
    us = u - s
    mm = r * us
    sd = s * dens
    dd = dbl * dens
    f_r = mm + sd
    f_n = mm * u + sd * sm + (pt - bn2)
    f_t = mm * t + sd * ts - bn * bt + dd * more_t
    f_w = mm * w + sd * ws - bn * bw + dd * more_w
    f_e = (energy * us + ptu - bn * vb + s * energy_star
           - dbl * ((dens * inv_root) * side_sg * more_work))
    f_bt = bt * us - bn * t + s * bts + dbl * more_bt
    f_bw = bw * us - bn * w + s * bws + dbl * more_bw
    return (f_r, f_n, f_t, f_w, f_e, f_bt, f_bw)


def order_of(normal):
    n = normal
    t = n % 3 + 1
    w = t % 3 + 1
    return (0, n, t, w, 4, n + 4, t + 4, w + 4)


def flux_slots(normal):
    o = order_of(normal)
    return (o[0], o[1], o[2], o[3], o[4], o[6], o[7])


def params(mib):
    return pltpu.CompilerParams(vmem_limit_bytes=mib * MIB)


def pack(fields):
    def kernel(fields_ref, units_ref, stage_ref, in_sems, out_sems):
        arriving = []
        for u, pair in enumerate(PAIRS):
            copy = pltpu.make_async_copy(
                fields_ref.at[:, pl.ds(2 * pair, 2)], stage_ref.at[u], in_sems.at[u])
            copy.start()
            arriving.append(copy)
        leaving = []
        for u, pair in enumerate(PAIRS):
            arriving[u].wait()
            for f in range(FIELDS):
                for r in range(2):
                    place = PLACE[BACK[(2 * pair + r + 2 * f) % HOLDERS]]
                    copy = pltpu.make_async_copy(
                        stage_ref.at[u, f, r], units_ref.at[place, u],
                        out_sems.at[(u * FIELDS + f) * 2 + r])
                    copy.start()
                    leaving.append(copy)
        for copy in leaving:
            copy.wait()

    return pl.pallas_call(
        kernel,
        out_shape=jax.ShapeDtypeStruct((HOLDERS, UNITS, CELLS, DEPTH), jnp.float32),
        in_specs=[HBM],
        out_specs=HBM,
        scratch_shapes=[
            pltpu.VMEM((UNITS, FIELDS, 2, CELLS, DEPTH), jnp.float32),
            pltpu.SemaphoreType.DMA((UNITS,)),
            pltpu.SemaphoreType.DMA((UNITS * FIELDS * 2,)),
        ],
        name="pack",
    )(fields)


def rotate_rings(pos, offsets, shift, rings, peak):
    blocks = RING // CELLS

    def kernel(pos_ref, offsets_ref, shift_ref, peak_ref, ring_ref, out_ref, wide_ref):
        parity = pos_ref[0] & 1
        group = pos_ref[1]
        shear = shift_ref[0]

        def send(unit, slot, amount):
            for b in range(blocks):
                wide_ref[slot, b * CELLS:(b + 1) * CELLS, :] = ring_ref[PLACE[b], unit]
            wide_ref[slot, RING:RING + CELLS, :] = ring_ref[PLACE[0], unit]
            wide_ref[slot, RING + CELLS:, :] = ring_ref[PLACE[1], unit, 0:8]
            low = (-amount) & 7
            for b in range(blocks):
                base = pl.multiple_of(((b * CELLS - amount) & (RING - 1)) - low, 8)
                block = wide_ref[slot, pl.ds(base, CELLS + 8), :]
                block = pltpu.roll(block, CELLS + 8 - low, 0)
                out_ref[HOLDER[b], slot * CELLS:(slot + 1) * CELLS, :] = block[0:CELLS]

        def amount_of(row):
            return offsets_ref[group * ROWS + row]

        for unit, pair in enumerate(PAIRS):
            send(unit, unit, amount_of(2 * pair + parity))
        last = group == GROUPS - 1
        row = jnp.where(last, ROWS - 2, 0) + parity
        send(jnp.where(last, 1, 0), UNITS, amount_of(row) + jnp.where(last, shear, -shear))

        @pl.when((group > 0) & (group < GROUPS - 1))
        def _():
            for b in range(blocks):
                out_ref[b, EXTRA:EXTRA + 8, :] = peak_ref[...]

    return pl.pallas_call(
        kernel,
        out_shape=jax.ShapeDtypeStruct((blocks, LINES, DEPTH), jnp.float32),
        in_specs=[SMEM, SMEM, SMEM, VMEM, VMEM],
        out_specs=VMEM,
        scratch_shapes=[pltpu.VMEM((UNITS + 1, RING + CELLS + 8, DEPTH), jnp.float32)],
        compiler_params=params(16),
        name="rotate",
    )(pos, offsets, shift, peak, rings)


def peak_of(blocks_ref):
    peak = blocks_ref[0, EXTRA:EXTRA + 8, :]
    for h in range(1, HOLDERS):
        peak = jnp.maximum(peak, blocks_ref[h, EXTRA:EXTRA + 8, :])
    return peak


def rims(pos, blocks):
    ghost = jax.ShapeDtypeStruct((GHOSTS + 8, DEPTH), jnp.float32)
    edge = jax.ShapeDtypeStruct((FIELDS, ROWS, 2, DEPTH), jnp.float32)

    def kernel(pos_ref, blocks_ref, az0_ref, az1_ref, rad0_ref, rad1_ref):
        group = pos_ref[1]
        rad_even = (group & 1) == 0
        az_even = pos_ref[2] == 0
        top_at = jnp.where(group == GROUPS - 1, EXTRA, CELLS)
        low_at = jnp.where(group == 0, EXTRA, 0)
        for f in range(FIELDS):
            for u, pair in enumerate(PAIRS):
                for r in range(2):
                    h = (2 * pair + r + 2 * f) % HOLDERS
                    right = blocks_ref[h, (u + 1) * CELLS - 2:(u + 1) * CELLS, :]
                    left = blocks_ref[h, u * CELLS:u * CELLS + 2, :]
                    az0_ref[f, 2 * pair + r] = jnp.where(az_even, right, left)
                    az1_ref[f, 2 * pair + r] = jnp.where(az_even, left, right)
            for r in range(2):
                top = (ROWS - 2 + r + 2 * f) % HOLDERS
                low = (r + 2 * f) % HOLDERS
                at = (2 * f + r) * CELLS
                for even, ref in ((True, rad0_ref), (False, rad1_ref)):
                    up = rad_even if even else jnp.logical_not(rad_even)
                    h = jnp.where(up, top, low)
                    start = pl.multiple_of(jnp.where(up, top_at, low_at), 8)
                    ref[at:at + CELLS, :] = blocks_ref[h, pl.ds(start, CELLS), :]
        peak = peak_of(blocks_ref)
        rad0_ref[GHOSTS:, :] = peak
        rad1_ref[GHOSTS:, :] = peak

    return pl.pallas_call(
        kernel,
        out_shape=(edge, edge, ghost, ghost),
        in_specs=[SMEM, VMEM],
        out_specs=(VMEM,) * 4,
        compiler_params=params(8),
        name="rims",
    )(pos, blocks)


PAD = 8
WIDE = 48
R_BLOCK = CELLS // 2


def unit_of(row):
    pair = row >> 1
    return jnp.where(pair < 4, 2 * pair, 15 - 2 * pair)


def load(blocks_ref, row, start, size):
    at = pl.multiple_of(unit_of(row) * CELLS + start, 8)
    return [blocks_ref[(row + 2 * f) & (HOLDERS - 1), pl.ds(at, size), :]
            for f in range(FIELDS)]


def vertical(blocks):
    order = order_of(3)
    slots = flux_slots(3)
    rows = ROWS

    def kernel(blocks_ref, acc_ref, left_ref, right_ref, flux_ref):
        def states(r):
            prim = to_primitive(load(blocks_ref, r, 0, CELLS))
            for k, f in enumerate(order):
                value = prim[f]
                below = pltpu.roll(value, 1, 1)
                above = pltpu.roll(value, DEPTH - 1, 1)
                beyond = pltpu.roll(value, DEPTH - 2, 1)
                step = above - value
                left_ref[k, r] = value + half_slope(value - below, step)
                right_ref[k, r] = above - half_slope(step, beyond - above)

        def fluxes(r):
            flux = hlld([left_ref[k, r] for k in range(8)], [right_ref[k, r] for k in range(8)])
            for k in range(7):
                flux_ref[k, r] = flux[k]

        def changes(r):
            state = load(blocks_ref, r, 0, CELLS)
            gains = [
                None,
                2.0 * OMEGA * state[2],
                -(2.0 - SHEAR) * OMEGA * state[1],
                None,
                SHEAR * OMEGA * (state[1] * state[2] / state[0] - state[5] * state[6]),
                None,
                -SHEAR * OMEGA * state[5],
                None,
            ]
            for k, slot in enumerate(slots):
                value = flux_ref[k, r]
                change = pltpu.roll(value, 1, 1) - value
                if gains[slot] is not None:
                    change = change + gains[slot]
                acc_ref[slot, r] = change

        states(0)

        def body(r, carry):
            changes(jnp.maximum(r - 1, 0))
            fluxes(r)
            states(jnp.minimum(r + 1, rows - 1))
            return carry

        lax.fori_loop(0, rows, body, 0)
        changes(rows - 1)

    sides = pltpu.VMEM((8, rows, CELLS, DEPTH), jnp.float32)
    return pl.pallas_call(
        kernel,
        out_shape=jax.ShapeDtypeStruct((FIELDS - 1, rows, CELLS, DEPTH), jnp.float32),
        in_specs=[VMEM],
        out_specs=VMEM,
        scratch_shapes=[sides, sides, sides],
        compiler_params=params(20),
        name="vertical",
    )(blocks)


def march(order, window, runs):
    def face(at, steps, lefts):
        new_steps, new_lefts, rights = [], [], []
        here, there = window(at), window(at + 1)
        for k, f in enumerate(order):
            step = there[f] - here[f]
            slope = half_slope(steps[k], step)
            rights.append(here[f] - slope)
            new_lefts.append(here[f] + slope)
            new_steps.append(step)
        return hlld(lefts, rights), new_steps, new_lefts

    a, b, c = window(-2), window(-1), window(0)
    steps = [c[f] - b[f] for f in order]
    lefts = [b[f] + half_slope(b[f] - a[f], step) for f, step in zip(order, steps)]
    lower, steps, lefts = face(0, steps, lefts)

    def body(emit, i, carry):
        lower, steps, lefts = carry
        upper, steps, lefts = face(i + 1, steps, lefts)
        emit(i, lower, upper)
        return (upper, steps, lefts)

    carry = (lower, steps, lefts)
    for start, stop, emit in runs:
        carry = lax.fori_loop(start, stop, functools.partial(body, emit), carry)


def fill(blocks_ref, prim_ref, top, start, size):
    def body(i, carry):
        values = to_primitive(load(blocks_ref, i, start, size))
        at = pl.multiple_of((i + top) * WIDE, 8) + PAD + start
        for f in range(FIELDS):
            prim_ref[f, pl.ds(at, size), :] = values[f]
        return carry

    lax.fori_loop(0, ROWS, body, 0)


def azimuthal(pos, blocks, edge0, edge1):
    def kernel(pos_ref, blocks_ref, edge0_ref, edge1_ref, turn_ref, prim_ref):
        even = pos_ref[2] == 0
        fill(blocks_ref, prim_ref, 0, 0, CELLS)

        def sides(i, carry):
            base = pl.multiple_of(i * WIDE, 8)
            first = [edge0_ref[f, i] for f in range(FIELDS)]
            second = [edge1_ref[f, i] for f in range(FIELDS)]
            for at, a, b in ((PAD - 2, second, first), (PAD + CELLS, first, second)):
                values = to_primitive([jnp.where(even, x, y) for x, y in zip(a, b)])
                for f in range(FIELDS):
                    prim_ref[f, pl.ds(base + at, 2), :] = values[f]
            return carry

        lax.fori_loop(0, ROWS, sides, 0, unroll=4)

        def rows_at(a):
            return [jnp.concatenate([
                prim_ref[f, pl.ds(g * WIDE + PAD + a, 8, stride=WIDE), :]
                for g in range(0, ROWS, 8)], axis=0) for f in range(FIELDS)]

        def keep(a, lower, upper):
            for k in range(7):
                turn_ref[k, pl.ds(pl.multiple_of(a * ROWS, 8), ROWS), :] = lower[k] - upper[k]

        march(order_of(2), rows_at, [(0, CELLS, keep)])

    return pl.pallas_call(
        kernel,
        out_shape=jax.ShapeDtypeStruct((7, CELLS * ROWS, DEPTH), jnp.float32),
        in_specs=[SMEM] + [VMEM] * 3,
        out_specs=VMEM,
        scratch_shapes=[pltpu.VMEM((FIELDS, ROWS * WIDE, DEPTH), jnp.float32)],
        compiler_params=params(12),
        name="azimuthal",
    )(pos, blocks, edge0, edge1)


def finish(pos, blocks, acc, turn, ghost0, ghost1):
    def kernel(pos_ref, blocks_ref, acc_ref, turn_ref, ghost0_ref, ghost1_ref,
               out_ref, prim_ref):
        group = pos_ref[1]
        even = (group & 1) == 0
        fill(blocks_ref, prim_ref, 2, 0, CELLS)
        for a_ref, b_ref, row in ((ghost1_ref, ghost0_ref, 0), (ghost0_ref, ghost1_ref, ROWS + 2)):
            for r in range(2):
                values = to_primitive([
                    jnp.where(even, a_ref[(2 * f + r) * CELLS:(2 * f + r + 1) * CELLS, :],
                              b_ref[(2 * f + r) * CELLS:(2 * f + r + 1) * CELLS, :])
                    for f in range(FIELDS)])
                at = (row + r) * WIDE + PAD
                for f in range(FIELDS):
                    prim_ref[f, at:at + CELLS, :] = values[f]

        a_slots = flux_slots(2)
        slots = flux_slots(1)
        peak = jnp.where((group == 0) | (group == GROUPS - 1),
                         ghost0_ref[GHOSTS:, :], peak_of(blocks_ref))
        dt = CFL_NUMBER / peak[0:1]

        for start in (0, R_BLOCK):
            part = slice(start, start + R_BLOCK)

            def cells_at(i):
                at = pl.multiple_of((i + 2) * WIDE, 8) + PAD + start
                return [prim_ref[f, pl.ds(at, R_BLOCK), :] for f in range(FIELDS)]

            def update(i, lower, upper):
                state = load(blocks_ref, i, start, R_BLOCK)
                change = [None] * FIELDS
                for k, slot in enumerate(slots):
                    change[slot] = lower[k] - upper[k]
                for k, slot in enumerate(a_slots):
                    turn = jnp.concatenate([
                        turn_ref[k, pl.ds((start + g) * ROWS + i, 8, stride=ROWS), :]
                        for g in range(0, R_BLOCK, 8)], axis=0)
                    change[slot] = turn if change[slot] is None else change[slot] + turn
                for slot in range(FIELDS - 1):
                    total = acc_ref[slot, i, part, :]
                    total = total if change[slot] is None else total + change[slot]
                    out_ref[slot, i, part, :] = state[slot] + dt * total
                out_ref[7, i, part, :] = state[7] + dt * change[7]

            march(order_of(1), cells_at, [(0, ROWS, update)])

    return pl.pallas_call(
        kernel,
        out_shape=jax.ShapeDtypeStruct((FIELDS, ROWS, CELLS, DEPTH), jnp.float32),
        in_specs=[SMEM] + [VMEM] * 5,
        out_specs=VMEM,
        scratch_shapes=[pltpu.VMEM((FIELDS, (ROWS + 4) * WIDE, DEPTH), jnp.float32)],
        compiler_params=params(20),
        name="finish",
    )(pos, blocks, acc, turn, ghost0, ghost1)


def over(peak, axis):
    for by in (1, 2, 4, 8):
        peak = jnp.maximum(peak, passed_along(peak, axis, by))
    return peak


def exchanged(units, order):
    return lax.all_to_all(units, AZ, split_axis=0, concat_axis=0, tiled=True,
                          axis_index_groups=[list(order)])


def local(fields, offsets, boundary_shift):
    holder = jnp.take(jnp.array(HOLDER, jnp.int32), lax.axis_index(AZ))
    az = lax.axis_index(AZ).astype(jnp.int32)
    pos = jnp.stack([holder, lax.axis_index(RAD).astype(jnp.int32), az & 1])
    rings = exchanged(pack(fields), ORDER)
    peak = jnp.broadcast_to(jnp.max(cell_speed(to_primitive(fields))), (8, DEPTH))
    peak = over(peak, RAD)
    blocks = exchanged(rotate_rings(pos, offsets, boundary_shift, rings, peak), BACK)
    az0, az1, rad0, rad1 = rims(pos, blocks)
    edge0 = swapped(az0, AZ, 0)
    edge1 = swapped(az1, AZ, 1)
    ghost0 = swapped(rad0, RAD, 0)
    ghost1 = swapped(rad1, RAD, 1)
    acc = vertical(blocks)
    turn = azimuthal(pos, blocks, edge0, edge1)
    return finish(pos, blocks, acc, turn, ghost0, ghost1)


def swapped(array, axis, odd):
    devices = lax.axis_size(axis)
    return lax.ppermute(array, axis, [
        (i, (i + (1 if (i + odd) % 2 == 0 else -1)) % devices) for i in range(devices)])


def solution(mesh):
    return jax.shard_map(
        local,
        mesh=mesh,
        in_specs=(P(None, RAD, AZ, None), P(), P()),
        out_specs=P(None, RAD, AZ, None),
        check_vma=False,
    )
```

```python
import functools

import jax
import jax.numpy as jnp
from jax import lax
from jax.experimental import pallas as pl
from jax.experimental.pallas import tpu as pltpu
from jax.sharding import PartitionSpec as P


AZ = "az"
RAD = "rad"

GAMMA = 5.0 / 3.0
CFL_NUMBER = 0.4
OMEGA = 1.0
SHEAR = 1.5

FIELDS = 8
ROWS = 16
CELLS = 32
RING = 512
DEPTH = 128
GROUPS = 16
HOLDERS = 16
UNITS = 8
PAIRS = (0, 7, 1, 6, 2, 5, 3, 4)
EXTRA = UNITS * CELLS
LINES = EXTRA + CELLS
GHOSTS = FIELDS * 2 * CELLS
ORDER = tuple(2 * z + x for x in (0, 1) for z in (0, 7, 1, 6, 2, 5, 3, 4))
BACK = ORDER[::-1]
PLACE = tuple(ORDER.index(d) for d in range(HOLDERS))
HOLDER = tuple(BACK.index(d) for d in range(HOLDERS))
TINY = 1e-30
VMEM = pl.BlockSpec(memory_space=pltpu.VMEM)
SMEM = pl.BlockSpec(memory_space=pltpu.SMEM)
HBM = pl.BlockSpec(memory_space=pl.ANY)
MIB = 1024 * 1024


def passed_along(array, axis, by):
    devices = lax.axis_size(axis)
    return lax.ppermute(array, axis, [(i, (i + by) % devices) for i in range(devices)])


def to_primitive(state):
    density = state[0]
    inverse = 1.0 / density
    vx = state[1] * inverse
    vy = state[2] * inverse
    vz = state[3] * inverse
    kinetic = 0.5 * (state[1] * vx + state[2] * vy + state[3] * vz)
    magnetic = 0.5 * (state[5] * state[5] + state[6] * state[6] + state[7] * state[7])
    pressure = (GAMMA - 1.0) * (state[4] - kinetic - magnetic)
    return (density, vx, vy, vz, pressure, state[5], state[6], state[7])


def fast_speed(density, pressure, normal_field, field_sq):
    sound = (GAMMA * pressure + field_sq) / density
    spread = jnp.maximum(
        sound * sound
        - 4.0 * GAMMA * pressure * normal_field * normal_field / (density * density),
        0.0,
    )
    return jnp.sqrt(0.5 * (sound + jnp.sqrt(spread)))


def cell_speed(prim):
    field_sq = prim[5] * prim[5] + prim[6] * prim[6] + prim[7] * prim[7]
    total = jnp.abs(prim[1]) + fast_speed(prim[0], prim[4], prim[5], field_sq)
    total = total + jnp.abs(prim[2]) + fast_speed(prim[0], prim[4], prim[6], field_sq)
    return total + jnp.abs(prim[3]) + fast_speed(prim[0], prim[4], prim[7], field_sq)


def half_slope(before, after):
    return 0.5 * jnp.minimum(
        jnp.maximum(after, jnp.minimum(before, 0.0)), jnp.maximum(before, 0.0)
    )


def hlld(left, right):
    rl, ul, tl, wl, pl_, nl, btl, bwl = left
    rr, ur, tr, wr, pr_, nr, btr, bwr = right
    bn = 0.5 * (nl + nr)
    bn2 = bn * bn
    bn2_4 = (4.0 * GAMMA) * bn2

    def signal(r, p, bt, bw):
        b2 = bn2 + (bt * bt + bw * bw)
        h = GAMMA * p + b2
        square = jnp.maximum(h * h - p * bn2_4, TINY)
        return (h + square * lax.rsqrt(square)) * (1.0 / r), p + 0.5 * b2

    sig_l, ptl = signal(rl, pl_, btl, bwl)
    sig_r, ptr = signal(rr, pr_, btr, bwr)
    square = 0.5 * jnp.maximum(sig_l, sig_r)
    fastest = square * lax.rsqrt(square)
    lower = jnp.minimum(ul, ur) - fastest
    upper = jnp.maximum(ul, ur) + fastest
    rel_l = lower - ul
    rel_r = upper - ur
    ml = rl * rel_l
    mr = rr * rel_r
    guess = (mr * ur - ml * ul - ptr + ptl) * (1.0 / (mr - ml))
    margin = 0.1 * (upper - lower)
    sm = jnp.minimum(jnp.maximum(guess, lower + margin), upper - margin)
    press_star = ptl + ml * (sm - ul)

    def star(m, rel, outer, u, t, w, bt, bw):
        dist = outer - sm
        product = m * dist
        inv_div = 1.0 / jnp.maximum(product - bn2, 0.5 * product)
        k = (sm - u) * (bn * inv_div)
        factor = (m * rel - bn2) * inv_div
        dens = m * (1.0 / dist)
        return (dens, dens * lax.rsqrt(dens),
                t - bt * k, w - bw * k, bt * factor, bw * factor)

    dl, ql, tsl, wsl, btsl, bwsl = star(ml, rel_l, lower, ul, tl, wl, btl, bwl)
    dr, qr, tsr, wsr, btsr, bwsr = star(mr, rel_r, upper, ur, tr, wr, btr, bwr)
    inv_sum = 1.0 / (ql + qr)
    al = ql * inv_sum
    ar = qr * inv_sum

    pos = sm > 0.0

    def pick(a, b):
        return jnp.where(pos, a, b)

    sg = jnp.where(bn < 0.0, -1.0, 1.0)
    sgs = sg * inv_sum
    qqs = (ql * qr) * sgs
    side_sg = pick(-sg, sg)
    own, other = pick(ar, -al), pick(al, -ar)
    jump_t, jump_w = tsr - tsl, wsr - wsl
    jump_bt, jump_bw = btsr - btsl, bwsr - bwsl
    more_t = own * jump_t + sgs * jump_bt
    more_w = own * jump_w + sgs * jump_bw
    more_bt = other * jump_bt + qqs * jump_t
    more_bw = other * jump_bw + qqs * jump_w

    r, u, t, w, p = pick(rl, rr), pick(ul, ur), pick(tl, tr), pick(wl, wr), pick(pl_, pr_)
    bt, bw, pt, outer = pick(btl, btr), pick(bwl, bwr), pick(ptl, ptr), pick(lower, upper)
    dens = pick(dl, dr)
    ts, ws, bts, bws = pick(tsl, tsr), pick(wsl, wsr), pick(btsl, btsr), pick(bwsl, bwsr)
    inv_root = lax.rsqrt(dens)
    inner = sm + (bn * side_sg) * inv_root
    inside = jnp.logical_not(lower > 0.0)
    inner_pos = inner > 0.0
    s = jnp.where(inside & (inner_pos | (upper > 0.0)), outer, 0.0)
    dbl = jnp.where(inside & (inner_pos ^ pos), inner, 0.0)

    energy = pt + 0.5 * (p + r * (u * u + t * t + w * w))
    vb = u * bn + t * bt + w * bw
    work = sm * bn + ts * bts + ws * bws
    more_work = (ts * more_bt + more_t * (bts + more_bt)
                 + ws * more_bw + more_w * (bws + more_bw))
    ptu = pt * u
    energy_star = ((outer - u) * energy - ptu + press_star * sm + bn * (vb - work)) * (
        1.0 / (outer - sm))
    us = u - s
    mm = r * us
    sd = s * dens
    dd = dbl * dens
    f_r = mm + sd
    f_n = mm * u + sd * sm + (pt - bn2)
    f_t = mm * t + sd * ts - bn * bt + dd * more_t
    f_w = mm * w + sd * ws - bn * bw + dd * more_w
    f_e = (energy * us + ptu - bn * vb + s * energy_star
           - dbl * ((dens * inv_root) * side_sg * more_work))
    f_bt = bt * us - bn * t + s * bts + dbl * more_bt
    f_bw = bw * us - bn * w + s * bws + dbl * more_bw
    return (f_r, f_n, f_t, f_w, f_e, f_bt, f_bw)


def order_of(normal):
    n = normal
    t = n % 3 + 1
    w = t % 3 + 1
    return (0, n, t, w, 4, n + 4, t + 4, w + 4)


def flux_slots(normal):
    o = order_of(normal)
    return (o[0], o[1], o[2], o[3], o[4], o[6], o[7])


def params(mib):
    return pltpu.CompilerParams(vmem_limit_bytes=mib * MIB)


def pack(fields):
    def kernel(fields_ref, units_ref, stage_ref, in_sems, out_sems):
        arriving = []
        for u, pair in enumerate(PAIRS):
            copies = [pltpu.make_async_copy(
                fields_ref.at[:, 2 * pair + r], stage_ref.at[u, :, 1 - r], in_sems.at[2 * u + r])
                for r in range(2)]
            for copy in copies:
                copy.start()
            arriving.append(copies)
        leaving = []
        for u, pair in enumerate(PAIRS):
            for copy in arriving[u]:
                copy.wait()
            for f in range(FIELDS):
                place = PLACE[BACK[(2 * pair + 1 + 2 * f) % HOLDERS]]
                copy = pltpu.make_async_copy(
                    stage_ref.at[u, f], units_ref.at[pl.ds(place, 2), u],
                    out_sems.at[u * FIELDS + f])
                copy.start()
                leaving.append(copy)
        for copy in leaving:
            copy.wait()

    return pl.pallas_call(
        kernel,
        out_shape=jax.ShapeDtypeStruct((HOLDERS, UNITS, CELLS, DEPTH), jnp.float32),
        in_specs=[HBM],
        out_specs=HBM,
        scratch_shapes=[
            pltpu.VMEM((UNITS, FIELDS, 2, CELLS, DEPTH), jnp.float32),
            pltpu.SemaphoreType.DMA((2 * UNITS,)),
            pltpu.SemaphoreType.DMA((UNITS * FIELDS,)),
        ],
        name="pack",
    )(fields)


def rotate_rings(pos, offsets, shift, rings, peak):
    blocks = RING // CELLS

    def kernel(pos_ref, offsets_ref, shift_ref, peak_ref, ring_ref, out_ref, wide_ref):
        parity = pos_ref[0] & 1
        group = pos_ref[1]
        shear = shift_ref[0]

        def send(unit, slot, amount):
            for b in range(blocks):
                wide_ref[slot, b * CELLS:(b + 1) * CELLS, :] = ring_ref[PLACE[b], unit]
            wide_ref[slot, RING:RING + CELLS, :] = ring_ref[PLACE[0], unit]
            wide_ref[slot, RING + CELLS:, :] = ring_ref[PLACE[1], unit, 0:8]
            low = (-amount) & 7
            for b in range(blocks):
                base = pl.multiple_of(((b * CELLS - amount) & (RING - 1)) - low, 8)
                block = wide_ref[slot, pl.ds(base, CELLS + 8), :]
                block = pltpu.roll(block, CELLS + 8 - low, 0)
                out_ref[HOLDER[b], slot * CELLS:(slot + 1) * CELLS, :] = block[0:CELLS]

        def amount_of(row):
            return offsets_ref[group * ROWS + row]

        for unit, pair in enumerate(PAIRS):
            send(unit, unit, amount_of(2 * pair + parity))
        last = group == GROUPS - 1
        row = jnp.where(last, ROWS - 2, 0) + parity
        send(jnp.where(last, 1, 0), UNITS, amount_of(row) + jnp.where(last, shear, -shear))

        @pl.when((group > 0) & (group < GROUPS - 1))
        def _():
            for b in range(blocks):
                out_ref[b, EXTRA:EXTRA + 8, :] = peak_ref[...]

    return pl.pallas_call(
        kernel,
        out_shape=jax.ShapeDtypeStruct((blocks, LINES, DEPTH), jnp.float32),
        in_specs=[SMEM, SMEM, SMEM, VMEM, VMEM],
        out_specs=VMEM,
        scratch_shapes=[pltpu.VMEM((UNITS + 1, RING + CELLS + 8, DEPTH), jnp.float32)],
        compiler_params=params(16),
        name="rotate",
    )(pos, offsets, shift, peak, rings)


def peak_of(blocks_ref):
    peak = blocks_ref[0, EXTRA:EXTRA + 8, :]
    for h in range(1, HOLDERS):
        peak = jnp.maximum(peak, blocks_ref[h, EXTRA:EXTRA + 8, :])
    return peak


def rims(pos, blocks):
    ghost = jax.ShapeDtypeStruct((GHOSTS + 8, DEPTH), jnp.float32)
    edge = jax.ShapeDtypeStruct((FIELDS, ROWS, 2, DEPTH), jnp.float32)

    def kernel(pos_ref, blocks_ref, az0_ref, az1_ref, rad0_ref, rad1_ref):
        group = pos_ref[1]
        rad_even = (group & 1) == 0
        az_even = pos_ref[2] == 0
        top_at = jnp.where(group == GROUPS - 1, EXTRA, CELLS)
        low_at = jnp.where(group == 0, EXTRA, 0)
        for f in range(FIELDS):
            for u, pair in enumerate(PAIRS):
                for r in range(2):
                    h = (2 * pair + r + 2 * f) % HOLDERS
                    right = blocks_ref[h, (u + 1) * CELLS - 2:(u + 1) * CELLS, :]
                    left = blocks_ref[h, u * CELLS:u * CELLS + 2, :]
                    az0_ref[f, 2 * pair + r] = jnp.where(az_even, right, left)
                    az1_ref[f, 2 * pair + r] = jnp.where(az_even, left, right)
            for r in range(2):
                top = (ROWS - 2 + r + 2 * f) % HOLDERS
                low = (r + 2 * f) % HOLDERS
                at = (2 * f + r) * CELLS
                for even, ref in ((True, rad0_ref), (False, rad1_ref)):
                    up = rad_even if even else jnp.logical_not(rad_even)
                    h = jnp.where(up, top, low)
                    start = pl.multiple_of(jnp.where(up, top_at, low_at), 8)
                    ref[at:at + CELLS, :] = blocks_ref[h, pl.ds(start, CELLS), :]
        peak = peak_of(blocks_ref)
        rad0_ref[GHOSTS:, :] = peak
        rad1_ref[GHOSTS:, :] = peak

    return pl.pallas_call(
        kernel,
        out_shape=(edge, edge, ghost, ghost),
        in_specs=[SMEM, VMEM],
        out_specs=(VMEM,) * 4,
        compiler_params=params(8),
        name="rims",
    )(pos, blocks)


PAD = 8
WIDE = 48
R_BLOCK = CELLS // 2


def unit_of(row):
    pair = row >> 1
    return jnp.where(pair < 4, 2 * pair, 15 - 2 * pair)


def load(blocks_ref, row, start, size):
    at = pl.multiple_of(unit_of(row) * CELLS + start, 8)
    return [blocks_ref[(row + 2 * f) & (HOLDERS - 1), pl.ds(at, size), :]
            for f in range(FIELDS)]


def vertical(blocks):
    order = order_of(3)
    slots = flux_slots(3)
    rows = ROWS

    def kernel(blocks_ref, acc_ref, left_ref, right_ref, flux_ref):
        def states(r):
            prim = to_primitive(load(blocks_ref, r, 0, CELLS))
            for k, f in enumerate(order):
                value = prim[f]
                below = pltpu.roll(value, 1, 1)
                above = pltpu.roll(value, DEPTH - 1, 1)
                beyond = pltpu.roll(value, DEPTH - 2, 1)
                step = above - value
                left_ref[k, r] = value + half_slope(value - below, step)
                right_ref[k, r] = above - half_slope(step, beyond - above)

        def fluxes(r):
            flux = hlld([left_ref[k, r] for k in range(8)], [right_ref[k, r] for k in range(8)])
            for k in range(7):
                flux_ref[k, r] = flux[k]

        def changes(r):
            state = load(blocks_ref, r, 0, CELLS)
            gains = [
                None,
                2.0 * OMEGA * state[2],
                -(2.0 - SHEAR) * OMEGA * state[1],
                None,
                SHEAR * OMEGA * (state[1] * state[2] / state[0] - state[5] * state[6]),
                None,
                -SHEAR * OMEGA * state[5],
                None,
            ]
            for k, slot in enumerate(slots):
                value = flux_ref[k, r]
                change = pltpu.roll(value, 1, 1) - value
                if gains[slot] is not None:
                    change = change + gains[slot]
                acc_ref[slot, r] = change

        states(0)

        def body(r, carry):
            changes(jnp.maximum(r - 1, 0))
            fluxes(r)
            states(jnp.minimum(r + 1, rows - 1))
            return carry

        lax.fori_loop(0, rows, body, 0)
        changes(rows - 1)

    sides = pltpu.VMEM((8, rows, CELLS, DEPTH), jnp.float32)
    return pl.pallas_call(
        kernel,
        out_shape=jax.ShapeDtypeStruct((FIELDS - 1, rows, CELLS, DEPTH), jnp.float32),
        in_specs=[VMEM],
        out_specs=VMEM,
        scratch_shapes=[sides, sides, sides],
        compiler_params=params(20),
        name="vertical",
    )(blocks)


def march(order, window, runs):
    def face(at, steps, lefts):
        new_steps, new_lefts, rights = [], [], []
        here, there = window(at), window(at + 1)
        for k, f in enumerate(order):
            step = there[f] - here[f]
            slope = half_slope(steps[k], step)
            rights.append(here[f] - slope)
            new_lefts.append(here[f] + slope)
            new_steps.append(step)
        return hlld(lefts, rights), new_steps, new_lefts

    a, b, c = window(-2), window(-1), window(0)
    steps = [c[f] - b[f] for f in order]
    lefts = [b[f] + half_slope(b[f] - a[f], step) for f, step in zip(order, steps)]
    lower, steps, lefts = face(0, steps, lefts)

    def body(emit, i, carry):
        lower, steps, lefts = carry
        upper, steps, lefts = face(i + 1, steps, lefts)
        emit(i, lower, upper)
        return (upper, steps, lefts)

    carry = (lower, steps, lefts)
    for start, stop, emit in runs:
        carry = lax.fori_loop(start, stop, functools.partial(body, emit), carry)


def fill(blocks_ref, prim_ref, top, start, size):
    def body(i, carry):
        values = to_primitive(load(blocks_ref, i, start, size))
        at = pl.multiple_of((i + top) * WIDE, 8) + PAD + start
        for f in range(FIELDS):
            prim_ref[f, pl.ds(at, size), :] = values[f]
        return carry

    lax.fori_loop(0, ROWS, body, 0, unroll=4)


def azimuthal(pos, blocks, edge0, edge1):
    def kernel(pos_ref, blocks_ref, edge0_ref, edge1_ref, turn_ref, prim_ref):
        even = pos_ref[2] == 0
        fill(blocks_ref, prim_ref, 0, 0, CELLS)

        def sides(i, carry):
            base = pl.multiple_of(i * WIDE, 8)
            first = [edge0_ref[f, i] for f in range(FIELDS)]
            second = [edge1_ref[f, i] for f in range(FIELDS)]
            for at, a, b in ((PAD - 2, second, first), (PAD + CELLS, first, second)):
                values = to_primitive([jnp.where(even, x, y) for x, y in zip(a, b)])
                for f in range(FIELDS):
                    prim_ref[f, pl.ds(base + at, 2), :] = values[f]
            return carry

        lax.fori_loop(0, ROWS, sides, 0, unroll=4)

        def rows_at(a):
            return [jnp.concatenate([
                prim_ref[f, pl.ds(g * WIDE + PAD + a, 8, stride=WIDE), :]
                for g in range(0, ROWS, 8)], axis=0) for f in range(FIELDS)]

        def keep(a, lower, upper):
            for k in range(7):
                turn_ref[k, pl.ds(pl.multiple_of(a * ROWS, 8), ROWS), :] = lower[k] - upper[k]

        march(order_of(2), rows_at, [(0, CELLS, keep)])

    return pl.pallas_call(
        kernel,
        out_shape=jax.ShapeDtypeStruct((7, CELLS * ROWS, DEPTH), jnp.float32),
        in_specs=[SMEM] + [VMEM] * 3,
        out_specs=VMEM,
        scratch_shapes=[pltpu.VMEM((FIELDS, ROWS * WIDE, DEPTH), jnp.float32)],
        compiler_params=params(12),
        name="azimuthal",
    )(pos, blocks, edge0, edge1)


def finish(pos, blocks, acc, turn, ghost0, ghost1):
    def kernel(pos_ref, blocks_ref, acc_ref, turn_ref, ghost0_ref, ghost1_ref,
               out_ref, prim_ref, done_ref, sems):
        group = pos_ref[1]
        even = (group & 1) == 0
        leaving = []
        fill(blocks_ref, prim_ref, 2, 0, CELLS)
        for a_ref, b_ref, row in ((ghost1_ref, ghost0_ref, 0), (ghost0_ref, ghost1_ref, ROWS + 2)):
            for r in range(2):
                values = to_primitive([
                    jnp.where(even, a_ref[(2 * f + r) * CELLS:(2 * f + r + 1) * CELLS, :],
                              b_ref[(2 * f + r) * CELLS:(2 * f + r + 1) * CELLS, :])
                    for f in range(FIELDS)])
                at = (row + r) * WIDE + PAD
                for f in range(FIELDS):
                    prim_ref[f, at:at + CELLS, :] = values[f]

        a_slots = flux_slots(2)
        slots = flux_slots(1)
        peak = jnp.where((group == 0) | (group == GROUPS - 1),
                         ghost0_ref[GHOSTS:, :], peak_of(blocks_ref))
        dt = CFL_NUMBER / peak[0:1]

        for half, start in enumerate((0, R_BLOCK)):
            part = slice(start, start + R_BLOCK)

            def cells_at(i):
                at = pl.multiple_of((i + 2) * WIDE, 8) + PAD + start
                return [prim_ref[f, pl.ds(at, R_BLOCK), :] for f in range(FIELDS)]

            def update(i, lower, upper):
                state = load(blocks_ref, i, start, R_BLOCK)
                change = [None] * FIELDS
                for k, slot in enumerate(slots):
                    change[slot] = lower[k] - upper[k]
                for k, slot in enumerate(a_slots):
                    turn = jnp.concatenate([
                        turn_ref[k, pl.ds((start + g) * ROWS + i, 8, stride=ROWS), :]
                        for g in range(0, R_BLOCK, 8)], axis=0)
                    change[slot] = turn if change[slot] is None else change[slot] + turn
                for slot in range(FIELDS - 1):
                    total = acc_ref[slot, i, part, :]
                    total = total if change[slot] is None else total + change[slot]
                    done_ref[half, slot, i] = state[slot] + dt * total
                done_ref[half, 7, i] = state[7] + dt * change[7]

            march(order_of(1), cells_at, [(0, ROWS, update)])
            copy = pltpu.make_async_copy(
                done_ref.at[half], out_ref.at[:, :, pl.ds(start, R_BLOCK)], sems.at[half])
            copy.start()
            leaving.append(copy)

        for copy in leaving:
            copy.wait()

    return pl.pallas_call(
        kernel,
        out_shape=jax.ShapeDtypeStruct((FIELDS, ROWS, CELLS, DEPTH), jnp.float32),
        in_specs=[SMEM] + [VMEM] * 5,
        out_specs=HBM,
        scratch_shapes=[
            pltpu.VMEM((FIELDS, (ROWS + 4) * WIDE, DEPTH), jnp.float32),
            pltpu.VMEM((2, FIELDS, ROWS, R_BLOCK, DEPTH), jnp.float32),
            pltpu.SemaphoreType.DMA((2,)),
        ],
        compiler_params=params(20),
        name="finish",
    )(pos, blocks, acc, turn, ghost0, ghost1)


def over(peak, axis):
    for by in (1, 2, 4, 8):
        peak = jnp.maximum(peak, passed_along(peak, axis, by))
    return peak


def exchanged(units, order):
    return lax.all_to_all(units, AZ, split_axis=0, concat_axis=0, tiled=True,
                          axis_index_groups=[list(order)])


def local(fields, offsets, boundary_shift):
    holder = jnp.take(jnp.array(HOLDER, jnp.int32), lax.axis_index(AZ))
    az = lax.axis_index(AZ).astype(jnp.int32)
    pos = jnp.stack([holder, lax.axis_index(RAD).astype(jnp.int32), az & 1])
    rings = exchanged(pack(fields), ORDER)
    peak = jnp.broadcast_to(jnp.max(cell_speed(to_primitive(fields))), (8, DEPTH))
    peak = over(peak, RAD)
    blocks = exchanged(rotate_rings(pos, offsets, boundary_shift, rings, peak), BACK)
    az0, az1, rad0, rad1 = rims(pos, blocks)
    edge0 = swapped(az0, AZ, 0)
    edge1 = swapped(az1, AZ, 1)
    ghost0 = swapped(rad0, RAD, 0)
    ghost1 = swapped(rad1, RAD, 1)
    acc = vertical(blocks)
    turn = azimuthal(pos, blocks, edge0, edge1)
    return finish(pos, blocks, acc, turn, ghost0, ghost1)


def swapped(array, axis, odd):
    devices = lax.axis_size(axis)
    return lax.ppermute(array, axis, [
        (i, (i + (1 if (i + odd) % 2 == 0 else -1)) % devices) for i in range(devices)])


def solution(mesh):
    return jax.shard_map(
        local,
        mesh=mesh,
        in_specs=(P(None, RAD, AZ, None), P(), P()),
        out_specs=P(None, RAD, AZ, None),
        check_vma=False,
    )
```
